256 devices in a mesh: beam: 2 (over core), tx: 8 (over y, x_hi), ty: 8 (over z), dom: 2 (over x_lo).
Axes of the slice: x: 4 (x_hi: 2, x_lo: 2; x = x_hi * 2 + x_lo), y: 4, z: 8, core: 2. Of those that a mesh axis runs over, the one named last changes fastest.
Arguments:
- cell_row: int32 [2, 2097152], P('beam', ('tx', 'ty', 'dom')), may hold values from 0 to 254
- cell_col: int32 [2, 2097152], P('beam', ('tx', 'ty', 'dom')), may hold values from 0 to 254
- weights: float32 [2, 2097152], P('beam', ('tx', 'ty', 'dom')), may hold values from -6 to 6
- momenta: float32 [2, 2, 2097152], P('beam', None, ('tx', 'ty', 'dom')), may hold values from -6 to 6
Outputs:
- kicked: float32 [2, 2, 2097152], P('beam', None, ('tx', 'ty', 'dom'))
The draws below stay inside these ranges and needn't reach their ends.
Inputs may be any that keep to these rules, and one draw needn't show every extreme that they name: cell_row is a row within the tile of 256 rows that holds the macroparticle, which lies on a device of that tile; its cloud also covers the next row. cell_col is a column within the tile of 256 columns that holds the macroparticle; its cloud also covers the next column.
All inputs are finite; a program needn't handle non-finite values.
Results may differ from the reference program's by a relative error of at most 0.00005.
Values sent between devices are 32-bit elements; how exact they have to be, the bound alone decides.
A program may use at most 64 MiB of HBM per device.

```python
import jax
import jax.numpy as jnp
from jax import lax

GRID = 2048
P_DEV = 16384
PARTS_SIZE = 2097152
TILE_ROWS = 256
TILE_COLS = 256
N_TX = 8
N_TY = 8
N_DOM = 2


def place_ends(entries, rng, least, high):
    dims = entries.shape
    place = [jax.random.randint(jax.random.fold_in(rng, axis), (), 0, dims[axis]) for axis in range(len(dims))]
    entries = entries.at[tuple(place)].set(least)
    longest = dims.index(max(dims))
    place[longest] = (place[longest] + 1) % dims[longest]
    return entries.at[tuple(place)].set(high)


def shard_levels(key, extent, pieces, least, high):
    def one(dim, parts):
        heights = jax.random.uniform(jax.random.fold_in(jax.random.fold_in(key, 6), dim), (parts,), jnp.float32, least / len(pieces), high / len(pieces))
        return jnp.repeat(jnp.exp(heights), extent[dim] // parts).reshape((-1,) + (1,) * (len(extent) - dim - 1))

    factor_of = one(*pieces[0])
    for cut in pieces[1:]:
        factor_of = factor_of * one(*cut)
    return factor_of


def noise(rng, shape, spread, limit, shards=(), kind=jnp.bfloat16):
    factor_of = shard_levels(rng, shape, shards, -0.22, 0.18) if shards else 1.0
    entries = jax.random.normal(rng, shape, jnp.float32) * spread * factor_of
    return jnp.minimum(jnp.maximum(entries, -limit), limit).astype(kind)


def setup_inputs(seed: int = 0) -> dict:
    seeds = jax.random.split(jax.random.key(seed), 5)
    return {
        "cell_row": place_ends(jax.random.randint(seeds[0], (2, PARTS_SIZE), 0, TILE_ROWS - 1), jax.random.fold_in(seeds[0], 1), 0, (TILE_ROWS - 1) - 1).astype(jnp.int32),
        "cell_col": place_ends(jax.random.randint(seeds[1], (2, PARTS_SIZE), 0, TILE_COLS - 1), jax.random.fold_in(seeds[1], 1), 0, (TILE_COLS - 1) - 1).astype(jnp.int32),
        "weights": noise(seeds[2], (2, PARTS_SIZE), 1.0, 6.0, ((0, 2), (1, 128)), jnp.float32),
        "momenta": noise(seeds[3], (2, 2, PARTS_SIZE), 1.0, 6.0, ((0, 2), (2, 128)), jnp.float32),
    }


highest = lax.Precision.HIGHEST
kick_gain = 2.0
row_weights = (0.75, 0.25)
col_weights = (0.625, 0.375)

def basis(family, position, wavenum, points):
    period = 2 * (points + 1)
    phase_idx = (position + 1) * (wavenum + 1) % period
    angles = jnp.pi * phase_idx.astype(jnp.float32) / (points + 1)
    scaling = jnp.sqrt(jnp.float32(2.0) / (points + 1))
    if family == 'sine':
        return scaling * jnp.sin(angles)
    wavenumber = jnp.pi * (wavenum + 1).astype(jnp.float32) / (points + 1)
    return -scaling * wavenumber * jnp.cos(angles)

def eigen_value(wavenum, points):
    halfsin = jnp.sin(jnp.pi * (wavenum + 1).astype(jnp.float32) / (2 * (points + 1)))
    return 4.0 * halfsin * halfsin

def green(row_modes, col_modes, points):
    return 1.0 / (eigen_value(row_modes, points) + eigen_value(col_modes, points))

def beam_fields(charge):
    modes = jnp.arange(GRID, dtype=jnp.int32)
    sine = basis('sine', modes[:, None], modes[None, :], GRID)
    slope = basis('slope', modes[:, None], modes[None, :], GRID)
    spectrum = jnp.dot(jnp.dot(sine, charge, precision=highest), sine, precision=highest)
    potential_hat = green(modes[:, None], modes[None, :], GRID) * spectrum
    along = jnp.dot(potential_hat, sine, precision=highest)
    across = jnp.dot(potential_hat, slope.T, precision=highest)
    field_x = jnp.dot(slope, along, precision=highest)
    field_y = jnp.dot(sine, across, precision=highest)
    return (field_x, field_y)

def global_cells(local_row, local_col):
    particle = jnp.arange(local_row.shape[0], dtype=jnp.int32)
    device = particle // P_DEV
    tile_x = device // (N_TY * N_DOM)
    tile_y = device // N_DOM % N_TY
    return (tile_x * (GRID // N_TX) + local_row, tile_y * (GRID // N_TY) + local_col)

def deposit(grid_row, grid_col, charges):
    charge = jnp.zeros((GRID, GRID), jnp.float32)
    for row_off in range(2):
        for col_off in range(2):
            amount = row_weights[row_off] * (col_weights[col_off] * charges)
            charge = charge.at[grid_row + row_off, grid_col + col_off].add(amount)
    return charge

def sample(field, grid_row, grid_col):
    result = jnp.zeros(grid_row.shape, jnp.float32)
    for row_off in range(2):
        for col_off in range(2):
            result = result + row_weights[row_off] * col_weights[col_off] * field[grid_row + row_off, grid_col + col_off]
    return result

def reference(cell_row, cell_col, weights, momenta):
    cells = [global_cells(cell_row[beam_no], cell_col[beam_no]) for beam_no in range(2)]
    fields = [beam_fields(deposit(cells[beam_no][0], cells[beam_no][1], weights[beam_no])) for beam_no in range(2)]
    kicks = []
    for beam_no in range(2):
        field_x, field_y = fields[1 - beam_no]
        grid_row, grid_col = cells[beam_no]
        kicks.append(jnp.stack([sample(field_x, grid_row, grid_col), sample(field_y, grid_row, grid_col)]))
    return momenta + kick_gain * jnp.stack(kicks)
```

```python
import jax
import jax.numpy as jnp
import numpy as np
from jax import lax
from jax.experimental import pallas as pl
from jax.experimental.pallas import tpu as pltpu
from jax.sharding import PartitionSpec as P

GRID = 2048
TILE = 256
BLOCKS = 8
SHARE = 16
PLANE = 16
RING = 8
HALF = 128
kick_gain = 2.0
f32 = jnp.float32
bf16 = jnp.bfloat16

COARSE_SIN, COARSE_COS, FINE_SIN, FINE_COS, CHUNK_SIN, CHUNK_COS, EIGEN, WAVE = (
    0, 16, 32, 48, 64, 72, 80, 81,
)
BASE_ROWS = 88


def base_tables():
    points = GRID + 1
    wave = np.arange(1, GRID + 1, dtype=np.int64)

    def angles(multiples):
        return np.pi * ((multiples[:, None] * wave[None, :]) % (2 * points)) / points

    coarse = angles(16 * np.arange(16, dtype=np.int64))
    fine = angles(np.arange(1, 17, dtype=np.int64))
    chunk = angles(TILE * np.arange(BLOCKS, dtype=np.int64))
    eigen = 4.0 * np.sin(np.pi * wave / (2 * points)) ** 2
    rows = np.zeros((BASE_ROWS, GRID))
    rows[0:80] = np.concatenate(
        [np.sin(coarse), np.cos(coarse), np.sin(fine), np.cos(fine), np.sin(chunk), np.cos(chunk)]
    )
    rows[EIGEN] = eigen
    rows[WAVE] = np.pi * wave / points
    blocks = rows.reshape(BASE_ROWS, BLOCKS, TILE).transpose(1, 0, 2)
    return np.ascontiguousarray(blocks).astype(np.float32)


def split(x):
    high = x.astype(bf16)
    low = (x - high.astype(f32)).astype(bf16)
    return high, low


def deposit_kernel(row_ref, col_ref, weight_ref, tile_ref, total):
    count = row_ref.shape[1]
    step = min(1024, count)
    total[...] = jnp.zeros_like(total)

    def body(i, carry):
        here = pl.ds(pl.multiple_of(i * step, step), step)
        cells = lax.broadcasted_iota(jnp.int32, (TILE, step), 0)
        weight = weight_ref[:, here]
        high = weight.astype(bf16).astype(f32)
        low = weight - high
        on_row = jnp.where(cells == row_ref[:, here], f32(1), f32(0)).astype(bf16)
        hit = cells == col_ref[:, here]
        on_col = jnp.concatenate(
            [
                jnp.where(hit, high, f32(0)).astype(bf16),
                jnp.where(hit, low, f32(0)).astype(bf16),
            ],
            axis=0,
        )
        total[...] += lax.dot_general(
            on_col, on_row, (((1,), (1,)), ((), ())), preferred_element_type=f32
        )
        return carry

    lax.fori_loop(0, count // step, body, 0)
    tile = total[0:TILE, :] + total[TILE : 2 * TILE, :]
    tile = 0.75 * tile + 0.25 * pltpu.roll(tile, 1, 1)
    tile_ref[...] = 0.625 * tile + 0.375 * pltpu.roll(tile, 1, 0)


def sample_kernel(row_ref, col_ref, momenta_ref, field_ref, out_ref, parts):
    count = row_ref.shape[1]
    step = min(1024, count)
    for comp in range(2):
        field = field_ref[comp]
        field = 0.75 * field + 0.25 * pltpu.roll(field, TILE - 1, 1)
        field = kick_gain * (0.625 * field + 0.375 * pltpu.roll(field, TILE - 1, 0))
        high, low = split(field)
        parts[comp * TILE : (comp + 1) * TILE, 0:TILE] = high
        parts[comp * TILE : (comp + 1) * TILE, TILE : 2 * TILE] = low

    def body(i, carry):
        here = pl.ds(pl.multiple_of(i * step, step), step)
        cells = lax.broadcasted_iota(jnp.int32, (TILE, step), 0)
        on_row = jnp.where(cells == row_ref[:, here], f32(1), f32(0)).astype(bf16)
        near = jnp.dot(
            parts[...], jnp.concatenate([on_row, on_row], axis=0), preferred_element_type=f32
        )
        hit = cells == col_ref[:, here]
        for comp in range(2):
            kick = jnp.sum(
                jnp.where(hit, near[comp * TILE : (comp + 1) * TILE], f32(0)),
                axis=0,
                keepdims=True,
            )
            out_ref[comp : comp + 1, here] = momenta_ref[comp : comp + 1, here] + kick
        return carry

    lax.fori_loop(0, count // step, body, 0)


def solve_kernel(
    tile_ref, base_ref, field_ref,
    tables, lines, charge_in, modes_out, modes_in, turned_out, spectrum_in, scaled,
    column_out, column_in, back_out, back_in, field_out,
    send_a, recv_a, send_b, recv_b, send_z, recv_z, send_c, recv_c, send_p, recv_p, send_d, recv_d,
):
    beam, tx = lax.axis_index("beam"), lax.axis_index("tx")
    ty, dom = lax.axis_index("ty"), lax.axis_index("dom")
    here = tx * 2 + dom
    here_x, here_y = lax.rem(here, 4), lax.div(here, 4)

    def plane_peer(offset):
        x = lax.rem(here_x + lax.rem(offset, 4), 4)
        y = lax.rem(here_y + lax.div(offset, 4), 4)
        return y * 4 + x

    def plane_id(peer):
        return {"tx": lax.div(peer, 2), "dom": lax.rem(peer, 2)}

    def ring_peer(offset):
        return lax.rem(ty + offset, RING)

    def each(first, last, act):
        def body(i, carry):
            act(i)
            return carry

        lax.fori_loop(first, last, body, 0)

    def copy(src, dst, send, recv, device):
        return pltpu.make_async_remote_copy(
            src_ref=src, dst_ref=dst, send_sem=send, recv_sem=recv,
            device_id=device, device_id_type=pl.DeviceIdType.MESH,
        )

    def copy_a(i):
        peer = plane_peer(i)
        return copy(
            tile_ref.at[peer], charge_in.at[dom, tx], send_a.at[i], recv_a.at[i],
            {"beam": 1 - beam, **plane_id(peer)},
        )

    def copy_b(i):
        peer = plane_peer(i)
        return copy(modes_out.at[peer], modes_in.at[here], send_b.at[i], recv_b.at[i], plane_id(peer))

    def copy_z(i):
        peer = ring_peer(i)
        return copy(turned_out.at[peer], spectrum_in.at[ty], send_z.at[i], recv_z.at[i], {"ty": peer})

    def copy_c(comp, i):
        peer = ring_peer(i)
        return copy(
            column_out.at[comp, peer], column_in.at[comp, ty],
            send_c.at[comp, i], recv_c.at[comp, i], {"ty": peer},
        )

    def copy_p(comp, i):
        peer = plane_peer(i)
        return copy(
            back_out.at[comp, peer], back_in.at[comp, here],
            send_p.at[comp, i], recv_p.at[comp, i], plane_id(peer),
        )

    def copy_d(comp, i):
        peer = plane_peer(i)
        return copy(
            field_out.at[comp, lax.div(peer, 2)], field_ref.at[comp, here],
            send_d.at[comp, i], recv_d.at[comp, i], plane_id(peer),
        )

    barrier = pltpu.get_barrier_semaphore()

    def greet(device):
        pl.semaphore_signal(
            barrier, inc=1, device_id=device, device_id_type=pl.DeviceIdType.MESH
        )

    each(0, PLANE, lambda i: greet({"beam": 1 - beam, **plane_id(plane_peer(i))}))
    each(1, PLANE, lambda i: greet(plane_id(plane_peer(i))))
    each(1, RING, lambda i: greet({"ty": ring_peer(i)}))
    pl.semaphore_wait(barrier, PLANE + PLANE - 1 + RING - 1)

    each(0, PLANE, lambda i: copy_a(i).start())

    def fill(j):
        fine_sin = base_ref[j, FINE_SIN : FINE_SIN + 16, :]
        fine_cos = base_ref[j, FINE_COS : FINE_COS + 16, :]
        for a in range(16):
            coarse_sin = base_ref[j, COARSE_SIN + a : COARSE_SIN + a + 1, :]
            coarse_cos = base_ref[j, COARSE_COS + a : COARSE_COS + a + 1, :]
            pair = (
                coarse_sin * fine_cos + coarse_cos * fine_sin,
                coarse_cos * fine_cos - coarse_sin * fine_sin,
            )
            for kind in range(2):
                high, low = split(pair[kind])
                tables[kind, j, 16 * a : 16 * a + 16, :] = high
                tables[kind, j, TILE + 16 * a : TILE + 16 * a + 16, :] = high
                tables[kind, j, 2 * TILE + 16 * a : 2 * TILE + 16 * a + 16, :] = low

    each(0, BLOCKS, fill)

    def load_lines(x):
        high, low = split(x.reshape(BLOCKS * SHARE, TILE))
        lines[:, 0:TILE] = high
        lines[:, TILE : 2 * TILE] = low
        lines[:, 2 * TILE : 3 * TILE] = high

    def transform(j, cosine):
        by_sin = jnp.dot(lines[...], tables[0, j], preferred_element_type=f32)
        by_cos = jnp.dot(lines[...], tables[1, j], preferred_element_type=f32)
        result = None
        for chunk in range(BLOCKS):
            rows = slice(SHARE * chunk, SHARE * chunk + SHARE)
            chunk_sin = base_ref[j, CHUNK_SIN + chunk : CHUNK_SIN + chunk + 1, :]
            chunk_cos = base_ref[j, CHUNK_COS + chunk : CHUNK_COS + chunk + 1, :]
            if cosine:
                term = chunk_cos * by_cos[rows] - chunk_sin * by_sin[rows]
            else:
                term = chunk_sin * by_cos[rows] + chunk_cos * by_sin[rows]
            result = term if result is None else result + term
        return result

    each(0, PLANE, lambda i: copy_a(i).wait_recv())
    load_lines(charge_in[0] + charge_in[1])

    def row_modes(j):
        modes = transform(j, False)
        modes_out[2 * j] = modes[:, 0:HALF]
        modes_out[2 * j + 1] = modes[:, HALF:TILE]

    each(0, BLOCKS, row_modes)
    each(1, PLANE, lambda i: copy_b(i).start())
    modes_in[here] = modes_out[here]
    each(1, PLANE, lambda i: copy_b(i).wait_recv())
    turned_out[...] = modes_in[...].reshape(TILE, HALF).T.reshape(RING, SHARE, TILE)
    each(1, RING, lambda i: copy_z(i).start())
    spectrum_in[ty] = turned_out[ty]

    first_mode = here * HALF + ty * SHARE
    lane = lax.broadcasted_iota(jnp.int32, (SHARE, TILE), 1)
    sublane = lax.broadcasted_iota(jnp.int32, (SHARE, TILE), 0)
    mine = lane == sublane + lax.rem(first_mode, TILE)
    my_block = lax.div(first_mode, TILE)

    def of_mine(row):
        values = base_ref[my_block, row : row + 1, :]
        return jnp.sum(jnp.where(mine, values, f32(0)), axis=1, keepdims=True)

    my_eigen, my_wave = of_mine(EIGEN), of_mine(WAVE)

    each(1, RING, lambda i: copy_z(i).wait_recv())
    load_lines(spectrum_in[...])
    scale = f32((2.0 / (GRID + 1)) ** 2)

    def column_modes(j):
        potential = transform(j, False) * scale / (my_eigen + base_ref[j, EIGEN : EIGEN + 1, :])
        scaled[0, j] = -my_wave * potential
        scaled[1, j] = -base_ref[j, WAVE : WAVE + 1, :] * potential

    each(0, BLOCKS, column_modes)

    for comp in range(2):
        load_lines(scaled[comp])

        def column_back(j, comp=comp):
            column_out[comp, j] = transform(j, comp == 1)

        each(0, BLOCKS, column_back)
        each(1, RING, lambda i, comp=comp: copy_c(comp, i).start())
        column_in[comp, ty] = column_out[comp, ty]

    for comp in range(2):
        each(1, RING, lambda i, comp=comp: copy_c(comp, i).wait_recv())
        back_out[comp] = column_in[comp].reshape(HALF, TILE).T.reshape(PLANE, SHARE, HALF)
        each(1, PLANE, lambda i, comp=comp: copy_p(comp, i).start())
        back_in[comp, here] = back_out[comp, here]

    for comp in range(2):
        each(1, PLANE, lambda i, comp=comp: copy_p(comp, i).wait_recv())
        load_lines(
            jnp.concatenate(
                [
                    jnp.concatenate([back_in[comp, 2 * j], back_in[comp, 2 * j + 1]], axis=1)
                    for j in range(BLOCKS)
                ],
                axis=0,
            )
        )

        def row_back(j, comp=comp):
            field_out[comp, j] = transform(j, comp == 0)

        each(0, BLOCKS, row_back)
        each(1, PLANE, lambda i, comp=comp: copy_d(comp, i).start())
        field_ref[comp, here] = field_out[comp, tx]

    for comp in range(2):
        each(1, PLANE, lambda i, comp=comp: copy_d(comp, i).wait_recv())
    each(0, PLANE, lambda i: copy_a(i).wait_send())
    each(1, PLANE, lambda i: copy_b(i).wait_send())
    each(1, RING, lambda i: copy_z(i).wait_send())
    for comp in range(2):
        each(1, RING, lambda i, comp=comp: copy_c(comp, i).wait_send())
        each(1, PLANE, lambda i, comp=comp: copy_p(comp, i).wait_send())
        each(1, PLANE, lambda i, comp=comp: copy_d(comp, i).wait_send())


vmem = pl.BlockSpec(memory_space=pltpu.VMEM)


def shards(cell_row, cell_col, weights, momenta):
    count = cell_row.shape[1]
    limit = 48 * 1024 * 1024
    tile = pl.pallas_call(
        deposit_kernel,
        out_shape=jax.ShapeDtypeStruct((TILE, TILE), f32),
        in_specs=[vmem] * 3,
        out_specs=vmem,
        scratch_shapes=[pltpu.VMEM((2 * TILE, TILE), f32)],
        compiler_params=pltpu.CompilerParams(vmem_limit_bytes=limit),
        name="deposit",
    )(cell_row, cell_col, weights)
    dma = pltpu.SemaphoreType.DMA
    field = pl.pallas_call(
        solve_kernel,
        out_shape=jax.ShapeDtypeStruct((2, PLANE, SHARE, TILE), f32),
        in_specs=[vmem] * 2,
        out_specs=vmem,
        scratch_shapes=[
            pltpu.VMEM((2, BLOCKS, 3 * TILE, TILE), bf16),
            pltpu.VMEM((BLOCKS * SHARE, 3 * TILE), bf16),
            pltpu.VMEM((2, BLOCKS, SHARE, TILE), f32),
            pltpu.VMEM((PLANE, SHARE, HALF), f32),
            pltpu.VMEM((PLANE, SHARE, HALF), f32),
            pltpu.VMEM((RING, SHARE, TILE), f32),
            pltpu.VMEM((RING, SHARE, TILE), f32),
            pltpu.VMEM((2, BLOCKS, SHARE, TILE), f32),
            pltpu.VMEM((2, RING, SHARE, TILE), f32),
            pltpu.VMEM((2, RING, SHARE, TILE), f32),
            pltpu.VMEM((2, PLANE, SHARE, HALF), f32),
            pltpu.VMEM((2, PLANE, SHARE, HALF), f32),
            pltpu.VMEM((2, BLOCKS, SHARE, TILE), f32),
            dma((PLANE,)), dma((PLANE,)),
            dma((PLANE,)), dma((PLANE,)),
            dma((RING,)), dma((RING,)),
            dma((2, RING)), dma((2, RING)),
            dma((2, PLANE)), dma((2, PLANE)),
            dma((2, PLANE)), dma((2, PLANE)),
        ],
        compiler_params=pltpu.CompilerParams(
            vmem_limit_bytes=limit, collective_id=0, has_side_effects=True
        ),
        name="solve",
    )(tile.reshape(PLANE, SHARE, TILE), jnp.asarray(base_tables()))
    kicked = pl.pallas_call(
        sample_kernel,
        out_shape=jax.ShapeDtypeStruct((2, count), f32),
        in_specs=[vmem] * 4,
        out_specs=vmem,
        scratch_shapes=[pltpu.VMEM((2 * TILE, 2 * TILE), bf16)],
        compiler_params=pltpu.CompilerParams(vmem_limit_bytes=limit),
        name="sample",
    )(cell_row, cell_col, momenta[0], field.reshape(2, TILE, TILE))
    return kicked[None]


def solution(mesh):
    placed = (
        P("beam", ("tx", "ty", "dom")),
        P("beam", ("tx", "ty", "dom")),
        P("beam", ("tx", "ty", "dom")),
        P("beam", None, ("tx", "ty", "dom")),
    )
    return jax.shard_map(
        shards,
        mesh=mesh,
        in_specs=placed,
        out_specs=P("beam", None, ("tx", "ty", "dom")),
        check_vma=False,
    )
```

```python
import jax
import jax.numpy as jnp
import numpy as np
from jax import lax
from jax.experimental import pallas as pl
from jax.experimental.pallas import tpu as pltpu
from jax.sharding import PartitionSpec as P

GRID = 2048
TILE = 256
BLOCKS = 8
SHARE = 16
PLANE = 16
RING = 8
HALF = 128
DEPOSIT_STEP = 4096
SAMPLE_STEP = 2048
kick_gain = 2.0
f32 = jnp.float32
bf16 = jnp.bfloat16

COARSE_SIN, COARSE_COS, FINE_SIN, FINE_COS, CENTRE_SIN, CENTRE_COS, EIGEN, WAVE = (
    0, 8, 16, 32, 48, 56, 64, 65,
)
BASE_ROWS = 72


def base_tables():
    points = GRID + 1
    wave = np.arange(1, GRID + 1, dtype=np.int64)

    def angles(doubled):
        doubled = np.asarray(doubled, dtype=np.int64)
        return np.pi * ((doubled[:, None] * wave[None, :]) % (4 * points)) / (2 * points)

    coarse = angles(32 * np.arange(8))
    fine = angles(2 * np.arange(16) + 1)
    centre = angles(2 * TILE * np.arange(BLOCKS) + TILE + 1)
    rows = np.zeros((BASE_ROWS, GRID))
    rows[0:64] = np.concatenate(
        [np.sin(coarse), np.cos(coarse), np.sin(fine), np.cos(fine), np.sin(centre), np.cos(centre)]
    )
    rows[EIGEN] = 4.0 * np.sin(np.pi * wave / (2 * points)) ** 2
    rows[WAVE] = np.pi * wave / points
    blocks = rows.reshape(BASE_ROWS, BLOCKS, TILE).transpose(1, 0, 2)
    return np.ascontiguousarray(blocks).astype(np.float32)


def split(x):
    high = x.astype(bf16)
    low = (x - high.astype(f32)).astype(bf16)
    return high, low


def collide_kernel(
    row_hbm, col_hbm, weight_hbm, momenta_hbm, base_hbm, out_ref,
    row_ref, col_ref, weight_ref, momenta_ref, base_ref,
    on_rows, total, tile_out, tables, even, odd, charge_in, modes_out, modes_in, turned_out,
    spectrum_in, scaled, column_out, column_in, back_out, back_in, field_out, field_in, parts,
    load, send_a, recv_a, send_b, recv_b, send_z, recv_z, send_c, recv_c, send_p, recv_p,
    send_d, recv_d,
):
    beam, tx = lax.axis_index("beam"), lax.axis_index("tx")
    ty, dom = lax.axis_index("ty"), lax.axis_index("dom")
    here = tx * 2 + dom
    count = row_ref.shape[1]

    loads = [
        pltpu.make_async_copy(src, dst, load.at[i])
        for i, (src, dst) in enumerate(
            [
                (row_hbm, row_ref), (col_hbm, col_ref), (weight_hbm, weight_ref),
                (base_hbm, base_ref), (momenta_hbm, momenta_ref),
            ]
        )
    ]
    for item in loads:
        item.start()

    def each(first, last, act):
        def body(i, carry):
            act(i)
            return carry

        lax.fori_loop(first, last, body, 0)

    def plane_id(peer):
        return {"tx": lax.div(peer, 2), "dom": lax.rem(peer, 2)}

    def other_id(peer):
        return {"beam": 1 - beam, "tx": lax.div(peer, 2), "dom": lax.rem(peer, 2)}

    def ring_id(peer):
        return {"ty": peer}

    def plane_peer(i):
        return lax.rem(here + i, PLANE)

    def ring_peer(i):
        return lax.rem(ty + i, RING)

    def copy(src, dst, send, recv, device):
        return pltpu.make_async_remote_copy(
            src_ref=src, dst_ref=dst, send_sem=send, recv_sem=recv,
            device_id=device, device_id_type=pl.DeviceIdType.MESH,
        )

    def to_a(peer):
        return copy(
            tile_out.at[peer], charge_in.at[dom, tx], send_a.at[peer], recv_a.at[here],
            other_id(peer),
        )

    def from_a(peer):
        slot = charge_in.at[lax.rem(peer, 2), lax.div(peer, 2)]
        return copy(slot, slot, send_a.at[peer], recv_a.at[peer], other_id(peer))

    def to_b(peer):
        return copy(
            modes_out.at[peer], modes_in.at[here], send_b.at[peer], recv_b.at[here],
            plane_id(peer),
        )

    def from_b(peer):
        slot = modes_in.at[peer]
        return copy(slot, slot, send_b.at[peer], recv_b.at[peer], plane_id(peer))

    def to_z(peer):
        return copy(
            turned_out.at[peer], spectrum_in.at[ty], send_z.at[peer], recv_z.at[ty],
            ring_id(peer),
        )

    def from_z(peer):
        slot = spectrum_in.at[peer]
        return copy(slot, slot, send_z.at[peer], recv_z.at[peer], ring_id(peer))

    def to_c(comp, peer):
        return copy(
            column_out.at[comp, peer], column_in.at[comp, ty],
            send_c.at[comp, peer], recv_c.at[comp, ty], ring_id(peer),
        )

    def from_c(comp, peer):
        slot = column_in.at[comp, peer]
        return copy(slot, slot, send_c.at[comp, peer], recv_c.at[comp, peer], ring_id(peer))

    def to_p(comp, peer):
        return copy(
            back_out.at[comp, peer], back_in.at[comp, here],
            send_p.at[comp, peer], recv_p.at[comp, here], plane_id(peer),
        )

    def from_p(comp, peer):
        slot = back_in.at[comp, peer]
        return copy(slot, slot, send_p.at[comp, peer], recv_p.at[comp, peer], plane_id(peer))

    def to_d(comp, peer):
        return copy(
            field_out.at[comp, lax.div(peer, 2)], field_in.at[comp, here],
            send_d.at[comp, peer], recv_d.at[comp, here], plane_id(peer),
        )

    def from_d(comp, peer):
        slot = field_in.at[comp, peer]
        return copy(slot, slot, send_d.at[comp, peer], recv_d.at[comp, peer], plane_id(peer))

    barrier = pltpu.get_barrier_semaphore()

    def greet(device):
        pl.semaphore_signal(
            barrier, inc=1, device_id=device, device_id_type=pl.DeviceIdType.MESH
        )

    each(0, PLANE, lambda i: greet(other_id(plane_peer(i))))
    each(1, PLANE, lambda i: greet(plane_id(plane_peer(i))))
    each(1, RING, lambda i: greet(ring_id(ring_peer(i))))

    total[...] = jnp.zeros_like(total)
    for item in loads[0:3]:
        item.wait()
    step = min(DEPOSIT_STEP, count)

    def deposit(i):
        part = pl.ds(pl.multiple_of(i * step, step), step)
        cells = lax.broadcasted_iota(jnp.int32, (TILE, step), 0).astype(f32).astype(bf16)
        high, low = split(weight_ref[:, part])
        on_row = jnp.where(
            cells == row_ref[:, part].astype(f32).astype(bf16), bf16(1), bf16(0)
        )
        on_rows[:, part] = on_row
        hit = cells == col_ref[:, part].astype(f32).astype(bf16)
        on_col = jnp.concatenate(
            [jnp.where(hit, high, bf16(0)), jnp.where(hit, low, bf16(0))], axis=0
        )
        total[...] += lax.dot_general(
            on_col, on_row, (((1,), (1,)), ((), ())), preferred_element_type=f32
        )

    each(0, count // step, deposit)
    tile = total[0:TILE, :] + total[TILE : 2 * TILE, :]
    tile = 0.75 * tile + 0.25 * pltpu.roll(tile, 1, 1)
    tile = 0.625 * tile + 0.375 * pltpu.roll(tile, 1, 0)
    tile_out[...] = tile.reshape(PLANE, SHARE, TILE)

    pl.semaphore_wait(barrier, PLANE + PLANE - 1 + RING - 1)
    each(0, PLANE, lambda i: to_a(plane_peer(i)).start())

    loads[3].wait()

    def fill(j):
        fine_sin = base_ref[j, FINE_SIN : FINE_SIN + 16, :]
        fine_cos = base_ref[j, FINE_COS : FINE_COS + 16, :]
        for a in range(8):
            coarse_sin = base_ref[j, COARSE_SIN + a : COARSE_SIN + a + 1, :]
            coarse_cos = base_ref[j, COARSE_COS + a : COARSE_COS + a + 1, :]
            pair = (
                coarse_sin * fine_cos + coarse_cos * fine_sin,
                coarse_cos * fine_cos - coarse_sin * fine_sin,
            )
            for kind in range(2):
                high, low = split(pair[kind])
                tables[kind, j, 16 * a : 16 * a + 16, :] = high
                tables[kind, j, HALF + 16 * a : HALF + 16 * a + 16, :] = low

    each(0, BLOCKS, fill)
    even[HALF:TILE, HALF:TILE] = jnp.zeros((HALF, HALF), bf16)
    odd[HALF:TILE, HALF:TILE] = jnp.zeros((HALF, HALF), bf16)

    def load_lines(left, right):
        backward = (HALF - 1) - lax.broadcasted_iota(jnp.int32, (HALF, HALF), 1)
        left = jnp.take_along_axis(left, backward, axis=1)
        for ref, folded in ((even, right + left), (odd, right - left)):
            high, low = split(folded)
            ref[0:HALF, 0:HALF] = high
            ref[0:HALF, HALF:TILE] = high
            ref[HALF:TILE, 0:HALF] = low

    def load_chunks(x):
        x = x.reshape(BLOCKS * SHARE, TILE)
        load_lines(x[:, 0:HALF], x[:, HALF:TILE])

    def transform(j, cosine):
        by_sin = jnp.dot(odd[...], tables[0, j], preferred_element_type=f32)
        by_cos = jnp.dot(even[...], tables[1, j], preferred_element_type=f32)
        by_sin = by_sin[0:HALF] + by_sin[HALF:TILE]
        by_cos = by_cos[0:HALF] + by_cos[HALF:TILE]
        result = None
        for chunk in range(BLOCKS):
            rows = slice(SHARE * chunk, SHARE * chunk + SHARE)
            centre_sin = base_ref[j, CENTRE_SIN + chunk : CENTRE_SIN + chunk + 1, :]
            centre_cos = base_ref[j, CENTRE_COS + chunk : CENTRE_COS + chunk + 1, :]
            if cosine:
                term = centre_cos * by_cos[rows] - centre_sin * by_sin[rows]
            else:
                term = centre_sin * by_cos[rows] + centre_cos * by_sin[rows]
            result = term if result is None else result + term
        return result

    def send_plane(peer, start):
        @pl.when(peer != here)
        def _():
            start(peer)

    each(0, PLANE, lambda i: from_a(plane_peer(i)).wait_recv())
    load_chunks(charge_in[0] + charge_in[1])

    def row_modes(i):
        j = lax.rem(tx + 1 + i, BLOCKS)
        modes = transform(j, False)
        modes_out[2 * j] = modes[:, 0:HALF]
        modes_out[2 * j + 1] = modes[:, HALF:TILE]
        for peer in (2 * j, 2 * j + 1):
            send_plane(peer, lambda peer: to_b(peer).start())

    each(0, BLOCKS, row_modes)
    modes_in[here] = modes_out[here]

    first_mode = here * HALF + ty * SHARE
    lane = lax.broadcasted_iota(jnp.int32, (SHARE, TILE), 1)
    sublane = lax.broadcasted_iota(jnp.int32, (SHARE, TILE), 0)
    mine = lane == sublane + lax.rem(first_mode, TILE)
    my_block = lax.div(first_mode, TILE)

    def of_mine(row):
        values = base_ref[my_block, row : row + 1, :]
        return jnp.sum(jnp.where(mine, values, f32(0)), axis=1, keepdims=True)

    my_eigen, my_wave = of_mine(EIGEN), of_mine(WAVE)

    each(1, PLANE, lambda i: from_b(plane_peer(i)).wait_recv())
    turned_out[...] = modes_in[...].reshape(TILE, HALF).T.reshape(RING, SHARE, TILE)
    each(1, RING, lambda i: to_z(ring_peer(i)).start())
    spectrum_in[ty] = turned_out[ty]

    each(1, RING, lambda i: from_z(ring_peer(i)).wait_recv())
    load_chunks(spectrum_in[...])
    scale = f32((2.0 / (GRID + 1)) ** 2)

    def column_modes(j):
        potential = transform(j, False) * scale / (my_eigen + base_ref[j, EIGEN : EIGEN + 1, :])
        scaled[0, j] = -my_wave * potential
        scaled[1, j] = -base_ref[j, WAVE : WAVE + 1, :] * potential

    each(0, BLOCKS, column_modes)

    for comp in range(2):
        load_chunks(scaled[comp])

        def column_back(i, comp=comp):
            j = lax.rem(ty + 1 + i, BLOCKS)
            column_out[comp, j] = transform(j, comp == 1)

            @pl.when(j != ty)
            def _():
                to_c(comp, j).start()

        each(0, BLOCKS, column_back)
        column_in[comp, ty] = column_out[comp, ty]

    for comp in range(2):
        each(1, RING, lambda i, comp=comp: from_c(comp, ring_peer(i)).wait_recv())
        back_out[comp] = column_in[comp].reshape(HALF, TILE).T.reshape(PLANE, SHARE, HALF)
        each(1, PLANE, lambda i, comp=comp: to_p(comp, plane_peer(i)).start())
        back_in[comp, here] = back_out[comp, here]

    for comp in range(2):
        each(1, PLANE, lambda i, comp=comp: from_p(comp, plane_peer(i)).wait_recv())
        load_lines(
            jnp.concatenate([back_in[comp, 2 * j] for j in range(BLOCKS)], axis=0),
            jnp.concatenate([back_in[comp, 2 * j + 1] for j in range(BLOCKS)], axis=0),
        )

        def row_back(i, comp=comp):
            j = lax.rem(tx + 1 + i, BLOCKS)
            field_out[comp, j] = transform(j, comp == 0)
            for peer in (2 * j, 2 * j + 1):
                send_plane(peer, lambda peer: to_d(comp, peer).start())

        each(0, BLOCKS, row_back)
        field_in[comp, here] = field_out[comp, tx]

    loads[4].wait()
    turn = min(SAMPLE_STEP, count)
    for comp in range(2):
        each(1, PLANE, lambda i, comp=comp: from_d(comp, plane_peer(i)).wait_recv())
        field = field_in[comp].reshape(TILE, TILE)
        field = 0.75 * field + 0.25 * pltpu.roll(field, TILE - 1, 1)
        field = kick_gain * (0.625 * field + 0.375 * pltpu.roll(field, TILE - 1, 0))
        high, low = split(field)
        parts[0:TILE, :] = high
        parts[TILE : 2 * TILE, :] = low

        def sample(i, comp=comp):
            part = pl.ds(pl.multiple_of(i * turn, turn), turn)
            cells = lax.broadcasted_iota(jnp.int32, (TILE, turn), 0)
            near = jnp.dot(parts[...], on_rows[:, part], preferred_element_type=f32)
            near = near[0:TILE] + near[TILE : 2 * TILE]
            kick = jnp.sum(
                jnp.where(cells == col_ref[:, part], near, f32(0)), axis=0, keepdims=True
            )
            out_ref[comp : comp + 1, part] = momenta_ref[comp : comp + 1, part] + kick

        each(0, count // turn, sample)

    each(0, PLANE, lambda i: to_a(plane_peer(i)).wait_send())
    each(1, PLANE, lambda i: to_b(plane_peer(i)).wait_send())
    each(1, RING, lambda i: to_z(ring_peer(i)).wait_send())
    for comp in range(2):
        each(1, RING, lambda i, comp=comp: to_c(comp, ring_peer(i)).wait_send())
        each(1, PLANE, lambda i, comp=comp: to_p(comp, plane_peer(i)).wait_send())
        each(1, PLANE, lambda i, comp=comp: to_d(comp, plane_peer(i)).wait_send())


def shards(cell_row, cell_col, weights, momenta):
    count = cell_row.shape[1]
    dma = pltpu.SemaphoreType.DMA
    base = base_tables()
    kicked = pl.pallas_call(
        collide_kernel,
        out_shape=jax.ShapeDtypeStruct((2, count), f32),
        in_specs=[pl.BlockSpec(memory_space=pltpu.HBM)] * 5,
        out_specs=pl.BlockSpec(memory_space=pltpu.VMEM),
        scratch_shapes=[
            pltpu.VMEM((1, count), jnp.int32),
            pltpu.VMEM((1, count), jnp.int32),
            pltpu.VMEM((1, count), f32),
            pltpu.VMEM((2, count), f32),
            pltpu.VMEM(base.shape, f32),
            pltpu.VMEM((TILE, count), bf16),
            pltpu.VMEM((2 * TILE, TILE), f32),
            pltpu.VMEM((PLANE, SHARE, TILE), f32),
            pltpu.VMEM((2, BLOCKS, TILE, TILE), bf16),
            pltpu.VMEM((TILE, TILE), bf16),
            pltpu.VMEM((TILE, TILE), bf16),
            pltpu.VMEM((2, BLOCKS, SHARE, TILE), f32),
            pltpu.VMEM((PLANE, SHARE, HALF), f32),
            pltpu.VMEM((PLANE, SHARE, HALF), f32),
            pltpu.VMEM((RING, SHARE, TILE), f32),
            pltpu.VMEM((RING, SHARE, TILE), f32),
            pltpu.VMEM((2, BLOCKS, SHARE, TILE), f32),
            pltpu.VMEM((2, RING, SHARE, TILE), f32),
            pltpu.VMEM((2, RING, SHARE, TILE), f32),
            pltpu.VMEM((2, PLANE, SHARE, HALF), f32),
            pltpu.VMEM((2, PLANE, SHARE, HALF), f32),
            pltpu.VMEM((2, BLOCKS, SHARE, TILE), f32),
            pltpu.VMEM((2, PLANE, SHARE, TILE), f32),
            pltpu.VMEM((2 * TILE, TILE), bf16),
            dma((5,)),
            dma((PLANE,)), dma((PLANE,)),
            dma((PLANE,)), dma((PLANE,)),
            dma((RING,)), dma((RING,)),
            dma((2, RING)), dma((2, RING)),
            dma((2, PLANE)), dma((2, PLANE)),
            dma((2, PLANE)), dma((2, PLANE)),
        ],
        compiler_params=pltpu.CompilerParams(
            vmem_limit_bytes=56 * 1024 * 1024, collective_id=0, has_side_effects=True
        ),
        name="collide",
    )(cell_row, cell_col, weights, momenta[0], jnp.asarray(base))
    return kicked[None]


def solution(mesh):
    placed = (
        P("beam", ("tx", "ty", "dom")),
        P("beam", ("tx", "ty", "dom")),
        P("beam", ("tx", "ty", "dom")),
        P("beam", None, ("tx", "ty", "dom")),
    )
    return jax.shard_map(
        shards,
        mesh=mesh,
        in_specs=placed,
        out_specs=P("beam", None, ("tx", "ty", "dom")),
        check_vma=False,
    )
```

```python
import jax
import jax.numpy as jnp
import numpy as np
from jax import lax
from jax.experimental import pallas as pl
from jax.experimental.pallas import tpu as pltpu
from jax.sharding import PartitionSpec as P

GRID = 2048
TILE = 256
BLOCKS = 8
SHARE = 16
PLANE = 16
RING = 8
HALF = 128
DEPOSIT_STEP = 8192
SAMPLE_STEP = 8192
kick_gain = 2.0
f32 = jnp.float32
bf16 = jnp.bfloat16

COARSE_SIN, COARSE_COS, FINE_SIN, FINE_COS, CENTRE_SIN, CENTRE_COS, EIGEN, WAVE = (
    0, 8, 16, 32, 48, 56, 64, 65,
)
BASE_ROWS = 72

EX_A, EX_B, EX_Z, EX_C, EX_P, EX_D, EXCHANGES = 0, 1, 2, 3, 5, 7, 9


def base_tables():
    points = GRID + 1
    wave = np.arange(1, GRID + 1, dtype=np.int64)

    def angles(doubled):
        doubled = np.asarray(doubled, dtype=np.int64)
        return np.pi * ((doubled[:, None] * wave[None, :]) % (4 * points)) / (2 * points)

    coarse = angles(32 * np.arange(8))
    fine = angles(2 * np.arange(16) + 1)
    centre = angles(2 * TILE * np.arange(BLOCKS) + TILE + 1)
    rows = np.zeros((BASE_ROWS, GRID))
    rows[0:64] = np.concatenate(
        [np.sin(coarse), np.cos(coarse), np.sin(fine), np.cos(fine), np.sin(centre), np.cos(centre)]
    )
    rows[EIGEN] = 4.0 * np.sin(np.pi * wave / (2 * points)) ** 2
    rows[WAVE] = np.pi * wave / points
    blocks = rows.reshape(BASE_ROWS, BLOCKS, TILE).transpose(1, 0, 2)
    return np.ascontiguousarray(blocks).astype(np.float32)


def split(x):
    high = x.astype(bf16)
    low = (x - high.astype(f32)).astype(bf16)
    return high, low


def collide_kernel(
    row_hbm, col_hbm, weight_hbm, momenta_hbm, base_hbm, out_hbm,
    row_ref, col_ref, weight_ref, momenta_ref, base_ref, out_ref,
    on_rows, total, tile_out, tables, even, odd, charge_in, modes_out, modes_in, turned_out,
    spectrum_in, scaled, column_out, column_in, back_out, back_in, field_out, field_in, parts,
    load, sent, came,
):
    beam, tx = lax.axis_index("beam"), lax.axis_index("tx")
    ty, dom = lax.axis_index("ty"), lax.axis_index("dom")
    here = tx * 2 + dom
    count = row_ref.shape[1]

    loads = [
        pltpu.make_async_copy(src, dst, load.at[i])
        for i, (src, dst) in enumerate(
            [
                (row_hbm, row_ref), (col_hbm, col_ref), (weight_hbm, weight_ref),
                (base_hbm, base_ref), (momenta_hbm, momenta_ref),
            ]
        )
    ]
    for item in loads:
        item.start()

    def each(first, last, act):
        def body(i, carry):
            act(i)
            return carry

        lax.fori_loop(first, last, body, 0)

    def plane_id(peer):
        return {"tx": lax.div(peer, 2), "dom": lax.rem(peer, 2)}

    def other_id(peer):
        return {"beam": 1 - beam, "tx": lax.div(peer, 2), "dom": lax.rem(peer, 2)}

    def ring_id(peer):
        return {"ty": peer}

    def plane_peer(i):
        return lax.rem(here + i, PLANE)

    def ring_peer(i):
        return lax.rem(ty + i, RING)

    def copy(src, dst, exchange, device):
        return pltpu.make_async_remote_copy(
            src_ref=src, dst_ref=dst, send_sem=sent.at[exchange], recv_sem=came.at[exchange],
            device_id=device, device_id_type=pl.DeviceIdType.MESH,
        )

    def to_a(peer):
        return copy(tile_out.at[peer], charge_in.at[dom, tx], EX_A, other_id(peer))

    def to_b(peer):
        return copy(modes_out.at[peer], modes_in.at[here], EX_B, plane_id(peer))

    def to_z(peer):
        return copy(turned_out.at[peer], spectrum_in.at[ty], EX_Z, ring_id(peer))

    def to_c(comp, peer):
        return copy(
            column_out.at[comp, peer], column_in.at[comp, ty], EX_C + comp, ring_id(peer)
        )

    def to_p(comp, peer):
        return copy(back_out.at[comp, peer], back_in.at[comp, here], EX_P + comp, plane_id(peer))

    def to_d(comp, peer):
        return copy(
            field_out.at[comp, lax.div(peer, 2)], field_in.at[comp, here],
            EX_D + comp, plane_id(peer),
        )

    others, rest = pl.ds(0, PLANE - 1), pl.ds(0, RING - 1)

    def all_of(exchange, comp=0):
        slots = {
            EX_A: charge_in,
            EX_B: modes_in.at[others],
            EX_Z: spectrum_in.at[rest],
            EX_C: column_in.at[comp, rest],
            EX_P: back_in.at[comp, others],
            EX_D: field_in.at[comp, others],
        }[exchange]
        device = ring_id(ring_peer(1)) if exchange in (EX_Z, EX_C) else plane_id(plane_peer(1))
        return copy(slots, slots, exchange + comp, device)

    barrier = pltpu.get_barrier_semaphore()

    def greet(device):
        pl.semaphore_signal(
            barrier, inc=1, device_id=device, device_id_type=pl.DeviceIdType.MESH
        )

    each(0, PLANE, lambda i: greet(other_id(plane_peer(i))))
    each(1, PLANE, lambda i: greet(plane_id(plane_peer(i))))
    each(1, RING, lambda i: greet(ring_id(ring_peer(i))))

    total[...] = jnp.zeros_like(total)
    for item in loads[0:3]:
        item.wait()
    step = min(DEPOSIT_STEP, count)

    def deposit(i):
        part = pl.ds(pl.multiple_of(i * step, step), step)
        cells = lax.broadcasted_iota(jnp.int32, (TILE, step), 0).astype(f32).astype(bf16)
        high, low = split(weight_ref[:, part])
        on_row = jnp.where(
            cells == row_ref[:, part].astype(f32).astype(bf16), bf16(1), bf16(0)
        )
        on_rows[:, part] = on_row
        hit = cells == col_ref[:, part].astype(f32).astype(bf16)
        on_col = jnp.concatenate(
            [jnp.where(hit, high, bf16(0)), jnp.where(hit, low, bf16(0))], axis=0
        )
        total[...] += lax.dot_general(
            on_col, on_row, (((1,), (1,)), ((), ())), preferred_element_type=f32
        )

    each(0, count // step, deposit)
    tile = total[0:TILE, :] + total[TILE : 2 * TILE, :]
    tile = 0.75 * tile + 0.25 * pltpu.roll(tile, 1, 1)
    tile = 0.625 * tile + 0.375 * pltpu.roll(tile, 1, 0)
    tile_out[...] = tile.reshape(PLANE, SHARE, TILE)

    pl.semaphore_wait(barrier, PLANE + PLANE - 1 + RING - 1)
    each(0, PLANE, lambda i: to_a(plane_peer(i)).start())

    loads[3].wait()

    def fill(j):
        fine_sin = base_ref[j, FINE_SIN : FINE_SIN + 16, :]
        fine_cos = base_ref[j, FINE_COS : FINE_COS + 16, :]
        for a in range(8):
            coarse_sin = base_ref[j, COARSE_SIN + a : COARSE_SIN + a + 1, :]
            coarse_cos = base_ref[j, COARSE_COS + a : COARSE_COS + a + 1, :]
            pair = (
                coarse_sin * fine_cos + coarse_cos * fine_sin,
                coarse_cos * fine_cos - coarse_sin * fine_sin,
            )
            for kind in range(2):
                high, low = split(pair[kind])
                tables[kind, j, 16 * a : 16 * a + 16, :] = high
                tables[kind, j, HALF + 16 * a : HALF + 16 * a + 16, :] = low

    each(0, BLOCKS, fill)
    even[HALF:TILE, HALF:TILE] = jnp.zeros((HALF, HALF), bf16)
    odd[HALF:TILE, HALF:TILE] = jnp.zeros((HALF, HALF), bf16)

    def load_lines(left, right):
        backward = (HALF - 1) - lax.broadcasted_iota(jnp.int32, (HALF, HALF), 1)
        left = jnp.take_along_axis(left, backward, axis=1)
        for ref, folded in ((even, right + left), (odd, right - left)):
            high, low = split(folded)
            ref[0:HALF, 0:HALF] = high
            ref[0:HALF, HALF:TILE] = high
            ref[HALF:TILE, 0:HALF] = low

    def load_chunks(x):
        x = x.reshape(BLOCKS * SHARE, TILE)
        load_lines(x[:, 0:HALF], x[:, HALF:TILE])

    def transform(j, cosine):
        by_sin = jnp.dot(odd[...], tables[0, j], preferred_element_type=f32)
        by_cos = jnp.dot(even[...], tables[1, j], preferred_element_type=f32)
        by_sin = by_sin[0:HALF] + by_sin[HALF:TILE]
        by_cos = by_cos[0:HALF] + by_cos[HALF:TILE]
        result = None
        for chunk in range(BLOCKS):
            rows = slice(SHARE * chunk, SHARE * chunk + SHARE)
            centre_sin = base_ref[j, CENTRE_SIN + chunk : CENTRE_SIN + chunk + 1, :]
            centre_cos = base_ref[j, CENTRE_COS + chunk : CENTRE_COS + chunk + 1, :]
            if cosine:
                term = centre_cos * by_cos[rows] - centre_sin * by_sin[rows]
            else:
                term = centre_sin * by_cos[rows] + centre_cos * by_sin[rows]
            result = term if result is None else result + term
        return result

    all_of(EX_A).wait_recv()
    load_chunks(charge_in[0] + charge_in[1])
    for j in range(BLOCKS):
        modes = transform(j, False)
        modes_out[2 * j] = modes[:, 0:HALF]
        modes_out[2 * j + 1] = modes[:, HALF:TILE]
    each(1, PLANE, lambda i: to_b(plane_peer(i)).start())
    modes_in[here] = modes_out[here]

    first_mode = here * HALF + ty * SHARE
    lane = lax.broadcasted_iota(jnp.int32, (SHARE, TILE), 1)
    sublane = lax.broadcasted_iota(jnp.int32, (SHARE, TILE), 0)
    mine = lane == sublane + lax.rem(first_mode, TILE)
    my_block = lax.div(first_mode, TILE)

    def of_mine(row):
        values = base_ref[my_block, row : row + 1, :]
        return jnp.sum(jnp.where(mine, values, f32(0)), axis=1, keepdims=True)

    my_eigen, my_wave = of_mine(EIGEN), of_mine(WAVE)

    all_of(EX_B).wait_recv()
    turned_out[...] = modes_in[...].reshape(TILE, HALF).T.reshape(RING, SHARE, TILE)
    each(1, RING, lambda i: to_z(ring_peer(i)).start())
    spectrum_in[ty] = turned_out[ty]

    all_of(EX_Z).wait_recv()
    load_chunks(spectrum_in[...])
    scale = f32((2.0 / (GRID + 1)) ** 2)
    for j in range(BLOCKS):
        potential = transform(j, False) * scale / (my_eigen + base_ref[j, EIGEN : EIGEN + 1, :])
        scaled[0, j] = -my_wave * potential
        scaled[1, j] = -base_ref[j, WAVE : WAVE + 1, :] * potential

    for comp in range(2):
        load_chunks(scaled[comp])
        for j in range(BLOCKS):
            column_out[comp, j] = transform(j, comp == 1)
        each(1, RING, lambda i, comp=comp: to_c(comp, ring_peer(i)).start())
        column_in[comp, ty] = column_out[comp, ty]

    for comp in range(2):
        all_of(EX_C, comp).wait_recv()
        back_out[comp] = column_in[comp].reshape(HALF, TILE).T.reshape(PLANE, SHARE, HALF)
        each(1, PLANE, lambda i, comp=comp: to_p(comp, plane_peer(i)).start())
        back_in[comp, here] = back_out[comp, here]

    for comp in range(2):
        all_of(EX_P, comp).wait_recv()
        load_lines(
            jnp.concatenate([back_in[comp, 2 * j] for j in range(BLOCKS)], axis=0),
            jnp.concatenate([back_in[comp, 2 * j + 1] for j in range(BLOCKS)], axis=0),
        )
        for j in range(BLOCKS):
            field_out[comp, j] = transform(j, comp == 0)
        each(1, PLANE, lambda i, comp=comp: to_d(comp, plane_peer(i)).start())
        field_in[comp, here] = field_out[comp, tx]

    loads[4].wait()
    turn = min(SAMPLE_STEP, count)
    for comp in range(2):
        all_of(EX_D, comp).wait_recv()
        field = field_in[comp].reshape(TILE, TILE)
        field = 0.75 * field + 0.25 * pltpu.roll(field, TILE - 1, 1)
        field = kick_gain * (0.625 * field + 0.375 * pltpu.roll(field, TILE - 1, 0))
        high, low = split(field)
        parts[0:TILE, :] = high
        parts[TILE : 2 * TILE, :] = low

        def sample(i, comp=comp):
            part = pl.ds(pl.multiple_of(i * turn, turn), turn)
            cells = lax.broadcasted_iota(jnp.int32, (TILE, turn), 0)
            near = jnp.dot(parts[...], on_rows[:, part], preferred_element_type=f32)
            near = near[0:TILE] + near[TILE : 2 * TILE]
            kick = jnp.sum(
                jnp.where(cells == col_ref[:, part], near, f32(0)), axis=0, keepdims=True
            )
            out_ref[comp : comp + 1, part] = momenta_ref[comp : comp + 1, part] + kick

        each(0, count // turn, sample)

    store = pltpu.make_async_copy(out_ref, out_hbm, load.at[0])
    store.start()
    for exchange in (EX_A, EX_B, EX_Z):
        all_of(exchange).wait_send()
    for comp in range(2):
        for exchange in (EX_C, EX_P, EX_D):
            all_of(exchange, comp).wait_send()
    store.wait()


def shards(cell_row, cell_col, weights, momenta):
    count = cell_row.shape[1]
    dma = pltpu.SemaphoreType.DMA
    base = base_tables()
    kicked = pl.pallas_call(
        collide_kernel,
        out_shape=jax.ShapeDtypeStruct((2, count), f32),
        in_specs=[pl.BlockSpec(memory_space=pltpu.HBM)] * 5,
        out_specs=pl.BlockSpec(memory_space=pltpu.HBM),
        scratch_shapes=[
            pltpu.VMEM((1, count), jnp.int32),
            pltpu.VMEM((1, count), jnp.int32),
            pltpu.VMEM((1, count), f32),
            pltpu.VMEM((2, count), f32),
            pltpu.VMEM(base.shape, f32),
            pltpu.VMEM((2, count), f32),
            pltpu.VMEM((TILE, count), bf16),
            pltpu.VMEM((2 * TILE, TILE), f32),
            pltpu.VMEM((PLANE, SHARE, TILE), f32),
            pltpu.VMEM((2, BLOCKS, TILE, TILE), bf16),
            pltpu.VMEM((TILE, TILE), bf16),
            pltpu.VMEM((TILE, TILE), bf16),
            pltpu.VMEM((2, BLOCKS, SHARE, TILE), f32),
            pltpu.VMEM((PLANE, SHARE, HALF), f32),
            pltpu.VMEM((PLANE, SHARE, HALF), f32),
            pltpu.VMEM((RING, SHARE, TILE), f32),
            pltpu.VMEM((RING, SHARE, TILE), f32),
            pltpu.VMEM((2, BLOCKS, SHARE, TILE), f32),
            pltpu.VMEM((2, RING, SHARE, TILE), f32),
            pltpu.VMEM((2, RING, SHARE, TILE), f32),
            pltpu.VMEM((2, PLANE, SHARE, HALF), f32),
            pltpu.VMEM((2, PLANE, SHARE, HALF), f32),
            pltpu.VMEM((2, BLOCKS, SHARE, TILE), f32),
            pltpu.VMEM((2, PLANE, SHARE, TILE), f32),
            pltpu.VMEM((2 * TILE, TILE), bf16),
            dma((5,)), dma((EXCHANGES,)), dma((EXCHANGES,)),
        ],
        compiler_params=pltpu.CompilerParams(
            vmem_limit_bytes=56 * 1024 * 1024, collective_id=0, has_side_effects=True
        ),
        name="collide",
    )(cell_row, cell_col, weights, momenta[0], jnp.asarray(base))
    return kicked[None]


def solution(mesh):
    placed = (
        P("beam", ("tx", "ty", "dom")),
        P("beam", ("tx", "ty", "dom")),
        P("beam", ("tx", "ty", "dom")),
        P("beam", None, ("tx", "ty", "dom")),
    )
    return jax.shard_map(
        shards,
        mesh=mesh,
        in_specs=placed,
        out_specs=P("beam", None, ("tx", "ty", "dom")),
        check_vma=False,
    )
```

```python
import jax
import jax.numpy as jnp
import numpy as np
from jax import lax
from jax.experimental import pallas as pl
from jax.experimental.pallas import tpu as pltpu
from jax.sharding import PartitionSpec as P

GRID = 2048
TILE = 256
BLOCKS = 8
SHARE = 16
PLANE = 16
RING = 8
HALF = 128
DEPOSIT_STEP = 8192
SAMPLE_STEP = 8192
kick_gain = 2.0
f32 = jnp.float32
bf16 = jnp.bfloat16

COARSE_SIN, COARSE_COS, FINE_SIN, FINE_COS, CENTRE_SIN, CENTRE_COS, EIGEN, WAVE = (
    0, 8, 16, 32, 48, 56, 64, 65,
)
BASE_ROWS = 72

EX_A, EX_B, EX_Z, EX_C, EX_P, EX_D, EXCHANGES = 0, 1, 2, 3, 5, 7, 9


def base_tables():
    points = GRID + 1
    wave = np.arange(1, GRID + 1, dtype=np.int64)

    def angles(doubled):
        doubled = np.asarray(doubled, dtype=np.int64)
        return np.pi * ((doubled[:, None] * wave[None, :]) % (4 * points)) / (2 * points)

    coarse = angles(32 * np.arange(8))
    fine = angles(2 * np.arange(16) + 1)
    centre = angles(2 * TILE * np.arange(BLOCKS) + TILE + 1)
    rows = np.zeros((BASE_ROWS, GRID))
    rows[0:64] = np.concatenate(
        [np.sin(coarse), np.cos(coarse), np.sin(fine), np.cos(fine), np.sin(centre), np.cos(centre)]
    )
    rows[EIGEN] = 4.0 * np.sin(np.pi * wave / (2 * points)) ** 2
    rows[WAVE] = np.pi * wave / points
    blocks = rows.reshape(BASE_ROWS, BLOCKS, TILE).transpose(1, 0, 2)
    return np.ascontiguousarray(blocks).astype(np.float32)


def split(x):
    high = x.astype(bf16)
    low = (x - high.astype(f32)).astype(bf16)
    return high, low


def collide_kernel(
    row_hbm, col_hbm, weight_hbm, momenta_hbm, base_hbm, out_ref,
    row_ref, col_ref, weight_ref, momenta_ref, base_ref,
    on_rows, total, tile_out, tables, even, odd, charge_in, modes_out, modes_in, turned_out,
    spectrum_in, scaled, column_out, column_in, back_out, back_in, field_out, field_in, parts,
    load, sent, came,
):
    beam, tx = lax.axis_index("beam"), lax.axis_index("tx")
    ty, dom = lax.axis_index("ty"), lax.axis_index("dom")
    here = tx * 2 + dom
    count = row_ref.shape[1]

    loads = [
        pltpu.make_async_copy(src, dst, load.at[i])
        for i, (src, dst) in enumerate(
            [
                (row_hbm, row_ref), (col_hbm, col_ref), (weight_hbm, weight_ref),
                (base_hbm, base_ref), (momenta_hbm, momenta_ref),
            ]
        )
    ]
    for item in loads:
        item.start()

    def each(first, last, act):
        def body(i, carry):
            act(i)
            return carry

        lax.fori_loop(first, last, body, 0)

    def plane_id(peer):
        return {"tx": lax.div(peer, 2), "dom": lax.rem(peer, 2)}

    def other_id(peer):
        return {"beam": 1 - beam, "tx": lax.div(peer, 2), "dom": lax.rem(peer, 2)}

    def ring_id(peer):
        return {"ty": peer}

    def hops(distance, size):
        return min(distance, size - distance)

    steps = [(dy, dx) for dy in range(4) for dx in range(4)]
    steps.sort(key=lambda step: -hops(step[0], 4) - hops(step[1], 4))
    plane_all = [
        lax.rem(lax.div(here, 4) + dy, 4) * 4 + lax.rem(lax.rem(here, 4) + dx, 4)
        for dy, dx in steps
    ]
    plane_others = plane_all[:-1]
    ring_others = [
        lax.rem(ty + step, RING)
        for step in sorted(range(1, RING), key=lambda step: -hops(step, RING))
    ]

    def copy(src, dst, exchange, device):
        return pltpu.make_async_remote_copy(
            src_ref=src, dst_ref=dst, send_sem=sent.at[exchange], recv_sem=came.at[exchange],
            device_id=device, device_id_type=pl.DeviceIdType.MESH,
        )

    def to_a(peer):
        return copy(tile_out.at[peer], charge_in.at[dom, tx], EX_A, other_id(peer))

    def to_b(peer):
        return copy(modes_out.at[peer], modes_in.at[here], EX_B, plane_id(peer))

    def to_z(peer):
        return copy(turned_out.at[peer], spectrum_in.at[ty], EX_Z, ring_id(peer))

    def to_c(comp, peer):
        return copy(
            column_out.at[comp, peer], column_in.at[comp, ty], EX_C + comp, ring_id(peer)
        )

    def to_p(comp, peer):
        return copy(back_out.at[comp, peer], back_in.at[comp, here], EX_P + comp, plane_id(peer))

    def to_d(comp, peer):
        return copy(
            field_out.at[comp, lax.div(peer, 2)], field_in.at[comp, here],
            EX_D + comp, plane_id(peer),
        )

    others, rest = pl.ds(0, PLANE - 1), pl.ds(0, RING - 1)

    def all_of(exchange, comp=0):
        slots = {
            EX_A: charge_in,
            EX_B: modes_in.at[others],
            EX_Z: spectrum_in.at[rest],
            EX_C: column_in.at[comp, rest],
            EX_P: back_in.at[comp, others],
            EX_D: field_in.at[comp, others],
        }[exchange]
        device = ring_id(ring_others[0]) if exchange in (EX_Z, EX_C) else plane_id(plane_others[0])
        return copy(slots, slots, exchange + comp, device)

    barrier = pltpu.get_barrier_semaphore()

    def greet(device):
        pl.semaphore_signal(
            barrier, inc=1, device_id=device, device_id_type=pl.DeviceIdType.MESH
        )

    for peer in plane_all:
        greet(other_id(peer))
    for peer in plane_others:
        greet(plane_id(peer))
    for peer in ring_others:
        greet(ring_id(peer))

    total[...] = jnp.zeros_like(total)
    for item in loads[0:3]:
        item.wait()
    step = min(DEPOSIT_STEP, count)

    def deposit(i):
        part = pl.ds(pl.multiple_of(i * step, step), step)
        cells = lax.broadcasted_iota(jnp.int32, (TILE, step), 0).astype(f32).astype(bf16)
        high, low = split(weight_ref[:, part])
        on_row = jnp.where(
            cells == row_ref[:, part].astype(f32).astype(bf16), bf16(1), bf16(0)
        )
        on_rows[:, part] = on_row
        hit = cells == col_ref[:, part].astype(f32).astype(bf16)
        on_col = jnp.concatenate(
            [jnp.where(hit, high, bf16(0)), jnp.where(hit, low, bf16(0))], axis=0
        )
        total[...] += lax.dot_general(
            on_col, on_row, (((1,), (1,)), ((), ())), preferred_element_type=f32
        )

    each(0, count // step, deposit)
    tile = total[0:TILE, :] + total[TILE : 2 * TILE, :]
    tile = 0.75 * tile + 0.25 * pltpu.roll(tile, 1, 1)
    tile = 0.625 * tile + 0.375 * pltpu.roll(tile, 1, 0)
    tile_out[...] = tile.reshape(PLANE, SHARE, TILE)

    pl.semaphore_wait(barrier, PLANE + PLANE - 1 + RING - 1)
    for peer in plane_all:
        to_a(peer).start()

    loads[3].wait()

    def fill(j):
        fine_sin = base_ref[j, FINE_SIN : FINE_SIN + 16, :]
        fine_cos = base_ref[j, FINE_COS : FINE_COS + 16, :]
        for a in range(8):
            coarse_sin = base_ref[j, COARSE_SIN + a : COARSE_SIN + a + 1, :]
            coarse_cos = base_ref[j, COARSE_COS + a : COARSE_COS + a + 1, :]
            pair = (
                coarse_sin * fine_cos + coarse_cos * fine_sin,
                coarse_cos * fine_cos - coarse_sin * fine_sin,
            )
            for kind in range(2):
                high, low = split(pair[kind])
                tables[kind, j, 16 * a : 16 * a + 16, :] = high
                tables[kind, j, HALF + 16 * a : HALF + 16 * a + 16, :] = low

    each(0, BLOCKS, fill)
    even[HALF:TILE, HALF:TILE] = jnp.zeros((HALF, HALF), bf16)
    odd[HALF:TILE, HALF:TILE] = jnp.zeros((HALF, HALF), bf16)

    def load_lines(left, right):
        backward = (HALF - 1) - lax.broadcasted_iota(jnp.int32, (HALF, HALF), 1)
        left = jnp.take_along_axis(left, backward, axis=1)
        for ref, folded in ((even, right + left), (odd, right - left)):
            high, low = split(folded)
            ref[0:HALF, 0:HALF] = high
            ref[0:HALF, HALF:TILE] = high
            ref[HALF:TILE, 0:HALF] = low

    def load_chunks(x):
        x = x.reshape(BLOCKS * SHARE, TILE)
        load_lines(x[:, 0:HALF], x[:, HALF:TILE])

    def transform(j, cosine):
        by_sin = jnp.dot(odd[...], tables[0, j], preferred_element_type=f32)
        by_cos = jnp.dot(even[...], tables[1, j], preferred_element_type=f32)
        by_sin = by_sin[0:HALF] + by_sin[HALF:TILE]
        by_cos = by_cos[0:HALF] + by_cos[HALF:TILE]
        result = None
        for chunk in range(BLOCKS):
            rows = slice(SHARE * chunk, SHARE * chunk + SHARE)
            centre_sin = base_ref[j, CENTRE_SIN + chunk : CENTRE_SIN + chunk + 1, :]
            centre_cos = base_ref[j, CENTRE_COS + chunk : CENTRE_COS + chunk + 1, :]
            if cosine:
                term = centre_cos * by_cos[rows] - centre_sin * by_sin[rows]
            else:
                term = centre_sin * by_cos[rows] + centre_cos * by_sin[rows]
            result = term if result is None else result + term
        return result

    all_of(EX_A).wait_recv()
    load_chunks(charge_in[0] + charge_in[1])
    for j in range(BLOCKS):
        modes = transform(j, False)
        modes_out[2 * j] = modes[:, 0:HALF]
        modes_out[2 * j + 1] = modes[:, HALF:TILE]
    for peer in plane_others:
        to_b(peer).start()
    modes_in[here] = modes_out[here]

    first_mode = here * HALF + ty * SHARE
    lane = lax.broadcasted_iota(jnp.int32, (SHARE, TILE), 1)
    sublane = lax.broadcasted_iota(jnp.int32, (SHARE, TILE), 0)
    mine = lane == sublane + lax.rem(first_mode, TILE)
    my_block = lax.div(first_mode, TILE)

    def of_mine(row):
        values = base_ref[my_block, row : row + 1, :]
        return jnp.sum(jnp.where(mine, values, f32(0)), axis=1, keepdims=True)

    my_eigen, my_wave = of_mine(EIGEN), of_mine(WAVE)

    all_of(EX_B).wait_recv()
    turned_out[...] = modes_in[...].reshape(TILE, HALF).T.reshape(RING, SHARE, TILE)
    for peer in ring_others:
        to_z(peer).start()
    spectrum_in[ty] = turned_out[ty]

    all_of(EX_Z).wait_recv()
    load_chunks(spectrum_in[...])
    scale = f32((2.0 / (GRID + 1)) ** 2)
    for j in range(BLOCKS):
        potential = transform(j, False) * scale / (my_eigen + base_ref[j, EIGEN : EIGEN + 1, :])
        scaled[0, j] = -my_wave * potential
        scaled[1, j] = -base_ref[j, WAVE : WAVE + 1, :] * potential

    for comp in range(2):
        load_chunks(scaled[comp])
        for j in range(BLOCKS):
            column_out[comp, j] = transform(j, comp == 1)
        for peer in ring_others:
            to_c(comp, peer).start()
        column_in[comp, ty] = column_out[comp, ty]

    for comp in range(2):
        all_of(EX_C, comp).wait_recv()
        back_out[comp] = column_in[comp].reshape(HALF, TILE).T.reshape(PLANE, SHARE, HALF)
        for peer in plane_others:
            to_p(comp, peer).start()
        back_in[comp, here] = back_out[comp, here]

    for comp in range(2):
        all_of(EX_P, comp).wait_recv()
        load_lines(
            jnp.concatenate([back_in[comp, 2 * j] for j in range(BLOCKS)], axis=0),
            jnp.concatenate([back_in[comp, 2 * j + 1] for j in range(BLOCKS)], axis=0),
        )
        for j in range(BLOCKS):
            field_out[comp, j] = transform(j, comp == 0)
        for peer in plane_others:
            to_d(comp, peer).start()
        field_in[comp, here] = field_out[comp, tx]

    loads[4].wait()
    turn = min(SAMPLE_STEP, count)
    for comp in range(2):
        all_of(EX_D, comp).wait_recv()
        field = field_in[comp].reshape(TILE, TILE)
        field = 0.75 * field + 0.25 * pltpu.roll(field, TILE - 1, 1)
        field = kick_gain * (0.625 * field + 0.375 * pltpu.roll(field, TILE - 1, 0))
        high, low = split(field)
        parts[0:TILE, :] = high
        parts[TILE : 2 * TILE, :] = low

        def sample(i, comp=comp):
            part = pl.ds(pl.multiple_of(i * turn, turn), turn)
            cells = lax.broadcasted_iota(jnp.int32, (TILE, turn), 0)
            near = jnp.dot(parts[...], on_rows[:, part], preferred_element_type=f32)
            near = near[0:TILE] + near[TILE : 2 * TILE]
            kick = jnp.sum(
                jnp.where(cells == col_ref[:, part], near, f32(0)), axis=0, keepdims=True
            )
            out_ref[comp : comp + 1, part] = momenta_ref[comp : comp + 1, part] + kick

        each(0, count // turn, sample)

    for exchange in (EX_A, EX_B, EX_Z):
        all_of(exchange).wait_send()
    for comp in range(2):
        for exchange in (EX_C, EX_P, EX_D):
            all_of(exchange, comp).wait_send()


def shards(cell_row, cell_col, weights, momenta):
    count = cell_row.shape[1]
    dma = pltpu.SemaphoreType.DMA
    base = base_tables()
    kicked = pl.pallas_call(
        collide_kernel,
        out_shape=jax.ShapeDtypeStruct((2, count), f32),
        in_specs=[pl.BlockSpec(memory_space=pltpu.HBM)] * 5,
        out_specs=pl.BlockSpec(memory_space=pltpu.VMEM),
        scratch_shapes=[
            pltpu.VMEM((1, count), jnp.int32),
            pltpu.VMEM((1, count), jnp.int32),
            pltpu.VMEM((1, count), f32),
            pltpu.VMEM((2, count), f32),
            pltpu.VMEM(base.shape, f32),
            pltpu.VMEM((TILE, count), bf16),
            pltpu.VMEM((2 * TILE, TILE), f32),
            pltpu.VMEM((PLANE, SHARE, TILE), f32),
            pltpu.VMEM((2, BLOCKS, TILE, TILE), bf16),
            pltpu.VMEM((TILE, TILE), bf16),
            pltpu.VMEM((TILE, TILE), bf16),
            pltpu.VMEM((2, BLOCKS, SHARE, TILE), f32),
            pltpu.VMEM((PLANE, SHARE, HALF), f32),
            pltpu.VMEM((PLANE, SHARE, HALF), f32),
            pltpu.VMEM((RING, SHARE, TILE), f32),
            pltpu.VMEM((RING, SHARE, TILE), f32),
            pltpu.VMEM((2, BLOCKS, SHARE, TILE), f32),
            pltpu.VMEM((2, RING, SHARE, TILE), f32),
            pltpu.VMEM((2, RING, SHARE, TILE), f32),
            pltpu.VMEM((2, PLANE, SHARE, HALF), f32),
            pltpu.VMEM((2, PLANE, SHARE, HALF), f32),
            pltpu.VMEM((2, BLOCKS, SHARE, TILE), f32),
            pltpu.VMEM((2, PLANE, SHARE, TILE), f32),
            pltpu.VMEM((2 * TILE, TILE), bf16),
            dma((5,)), dma((EXCHANGES,)), dma((EXCHANGES,)),
        ],
        compiler_params=pltpu.CompilerParams(
            vmem_limit_bytes=48 * 1024 * 1024, collective_id=0, has_side_effects=True
        ),
        name="collide",
    )(
        *[
            pltpu.with_memory_space_constraint(array, pltpu.HBM)
            for array in (cell_row, cell_col, weights, momenta[0], jnp.asarray(base))
        ]
    )
    return kicked[None]


def solution(mesh):
    placed = (
        P("beam", ("tx", "ty", "dom")),
        P("beam", ("tx", "ty", "dom")),
        P("beam", ("tx", "ty", "dom")),
        P("beam", None, ("tx", "ty", "dom")),
    )
    return jax.shard_map(
        shards,
        mesh=mesh,
        in_specs=placed,
        out_specs=P("beam", None, ("tx", "ty", "dom")),
        check_vma=False,
    )
```

```python
import jax
import jax.numpy as jnp
import numpy as np
from jax import lax
from jax.experimental import pallas as pl
from jax.experimental.pallas import tpu as pltpu
from jax.sharding import PartitionSpec as P

GRID = 2048
TILE = 256
BLOCKS = 8
SHARE = 16
PLANE = 16
RING = 8
HALF = 128
DEPOSIT_STEP = 8192
SAMPLE_STEP = 8192
ONE_HOT_STEP = 4096
kick_gain = 2.0
f32 = jnp.float32
bf16 = jnp.bfloat16

COARSE_SIN, COARSE_COS, FINE_SIN, FINE_COS, CENTRE_SIN, CENTRE_COS, EIGEN, WAVE = (
    0, 8, 16, 32, 48, 56, 64, 65,
)
BASE_ROWS = 72

EX_A, EX_B, EX_Z, EX_C, EX_P, EX_D, EX_CELLS, EX_KICK, EXCHANGES = 0, 1, 2, 3, 5, 7, 10, 12, 13


def base_tables():
    points = GRID + 1
    wave = np.arange(1, GRID + 1, dtype=np.int64)

    def angles(doubled):
        doubled = np.asarray(doubled, dtype=np.int64)
        return np.pi * ((doubled[:, None] * wave[None, :]) % (4 * points)) / (2 * points)

    coarse = angles(32 * np.arange(8))
    fine = angles(2 * np.arange(16) + 1)
    centre = angles(2 * TILE * np.arange(BLOCKS) + TILE + 1)
    rows = np.zeros((BASE_ROWS, GRID))
    rows[0:64] = np.concatenate(
        [np.sin(coarse), np.cos(coarse), np.sin(fine), np.cos(fine), np.sin(centre), np.cos(centre)]
    )
    rows[EIGEN] = 4.0 * np.sin(np.pi * wave / (2 * points)) ** 2
    rows[WAVE] = np.pi * wave / points
    blocks = rows.reshape(BASE_ROWS, BLOCKS, TILE).transpose(1, 0, 2)
    return np.ascontiguousarray(blocks).astype(np.float32)


def split(x):
    high = x.astype(bf16)
    low = (x - high.astype(f32)).astype(bf16)
    return high, low


def collide_kernel(
    row_hbm, col_hbm, weight_hbm, momenta_hbm, base_hbm, out_ref,
    row_ref, col_ref, weight_ref, momenta_ref, base_ref,
    row_two, col_two, kicks_two, kicks_in, rows_two, on_rows, total, tile_out, tables, even, odd, charge_in, modes_out, modes_in, turned_out,
    spectrum_in, scaled, column_out, column_in, back_out, back_in, field_out, field_in, parts,
    load, sent, came,
):
    beam, tx = lax.axis_index("beam"), lax.axis_index("tx")
    ty, dom = lax.axis_index("ty"), lax.axis_index("dom")
    here = tx * 2 + dom
    count = row_ref.shape[1]

    loads = [
        pltpu.make_async_copy(src, dst, load.at[i])
        for i, (src, dst) in enumerate(
            [
                (row_hbm, row_ref), (col_hbm, col_ref), (weight_hbm, weight_ref),
                (base_hbm, base_ref), (momenta_hbm, momenta_ref),
            ]
        )
    ]
    for item in loads:
        item.start()

    def each(first, last, act):
        def body(i, carry):
            act(i)
            return carry

        lax.fori_loop(first, last, body, 0)

    def plane_id(peer):
        return {"tx": lax.div(peer, 2), "dom": lax.rem(peer, 2)}

    def other_id(peer):
        return {"beam": 1 - beam, "tx": lax.div(peer, 2), "dom": lax.rem(peer, 2)}

    def ring_id(peer):
        return {"ty": peer}

    def hops(distance, size):
        return min(distance, size - distance)

    steps = [(dy, dx) for dy in range(4) for dx in range(4)]
    steps.sort(key=lambda step: -hops(step[0], 4) - hops(step[1], 4))
    plane_all = [
        lax.rem(lax.div(here, 4) + dy, 4) * 4 + lax.rem(lax.rem(here, 4) + dx, 4)
        for dy, dx in steps
    ]
    plane_others = plane_all[:-1]
    ring_others = [
        lax.rem(ty + step, RING)
        for step in sorted(range(1, RING), key=lambda step: -hops(step, RING))
    ]

    def copy(src, dst, exchange, device):
        return pltpu.make_async_remote_copy(
            src_ref=src, dst_ref=dst, send_sem=sent.at[exchange], recv_sem=came.at[exchange],
            device_id=device, device_id_type=pl.DeviceIdType.MESH,
        )

    mine_in = dom * BLOCKS + tx

    def to_a(peer):
        return copy(tile_out.at[peer], charge_in.at[mine_in], EX_A, plane_id(peer))

    def to_b(peer):
        return copy(modes_out.at[peer], modes_in.at[here], EX_B, plane_id(peer))

    def to_z(peer):
        return copy(turned_out.at[peer], spectrum_in.at[ty], EX_Z, ring_id(peer))

    def to_c(comp, peer):
        return copy(
            column_out.at[comp, peer], column_in.at[comp, ty], EX_C + comp, ring_id(peer)
        )

    def to_p(comp, peer):
        return copy(back_out.at[comp, peer], back_in.at[comp, here], EX_P + comp, plane_id(peer))

    def to_dx(peer):
        return copy(field_out.at[0, lax.div(peer, 2)], field_in.at[0, here], EX_D, other_id(peer))

    def to_dy(peer):
        return copy(
            field_out.at[1, lax.div(peer, 2)], field_in.at[1 + beam, here],
            EX_D + 1 + beam, {"beam": jnp.int32(1), **plane_id(peer)},
        )

    partner = {"beam": 1 - beam}
    cells_over = [
        copy(row_ref, row_two, EX_CELLS, partner), copy(col_ref, col_two, EX_CELLS + 1, partner)
    ]
    kicks_back = copy(kicks_two, kicks_in, EX_KICK, partner)

    others, rest = pl.ds(0, PLANE - 1), pl.ds(0, RING - 1)

    def all_of(exchange, comp=0):
        slots = {
            EX_A: charge_in.at[others],
            EX_B: modes_in.at[others],
            EX_Z: spectrum_in.at[rest],
            EX_C: column_in.at[comp, rest],
            EX_P: back_in.at[comp, others],
            EX_D: field_in.at[comp] if comp < 2 else field_in.at[comp, others],
        }[exchange]
        device = ring_id(ring_others[0]) if exchange in (EX_Z, EX_C) else plane_id(plane_others[0])
        return copy(slots, slots, exchange + comp, device)

    barrier = pltpu.get_barrier_semaphore()

    def greet(device):
        pl.semaphore_signal(
            barrier, inc=1, device_id=device, device_id_type=pl.DeviceIdType.MESH
        )

    for peer in plane_all:
        greet(other_id(peer))
    for peer in plane_others:
        greet(plane_id(peer))
    for peer in ring_others:
        greet(ring_id(peer))

    total[...] = jnp.zeros_like(total)
    for item in loads[0:3]:
        item.wait()
    step = min(DEPOSIT_STEP, count)

    def deposit(i):
        part = pl.ds(pl.multiple_of(i * step, step), step)
        cells = lax.broadcasted_iota(jnp.int32, (TILE, step), 0).astype(f32).astype(bf16)
        high, low = split(weight_ref[:, part])
        on_row = jnp.where(
            cells == row_ref[:, part].astype(f32).astype(bf16), bf16(1), bf16(0)
        )
        on_rows[:, part] = on_row
        hit = cells == col_ref[:, part].astype(f32).astype(bf16)
        on_col = jnp.concatenate(
            [jnp.where(hit, high, bf16(0)), jnp.where(hit, low, bf16(0))], axis=0
        )
        total[...] += lax.dot_general(
            on_col, on_row, (((1,), (1,)), ((), ())), preferred_element_type=f32
        )

    each(0, count // step, deposit)
    tile = total[0:TILE, :] + total[TILE : 2 * TILE, :]
    tile = 0.75 * tile + 0.25 * pltpu.roll(tile, 1, 1)
    tile = 0.625 * tile + 0.375 * pltpu.roll(tile, 1, 0)
    tile_out[...] = tile.reshape(PLANE, SHARE, TILE)

    pl.semaphore_wait(barrier, PLANE + PLANE - 1 + RING - 1)
    for peer in plane_others:
        to_a(peer).start()
    charge_in[mine_in] = tile_out[here]

    @pl.when(beam == 0)
    def _():
        for item in cells_over:
            item.start()


    loads[3].wait()

    def fill(j):
        fine_sin = base_ref[j, FINE_SIN : FINE_SIN + 16, :]
        fine_cos = base_ref[j, FINE_COS : FINE_COS + 16, :]
        for a in range(8):
            coarse_sin = base_ref[j, COARSE_SIN + a : COARSE_SIN + a + 1, :]
            coarse_cos = base_ref[j, COARSE_COS + a : COARSE_COS + a + 1, :]
            pair = (
                coarse_sin * fine_cos + coarse_cos * fine_sin,
                coarse_cos * fine_cos - coarse_sin * fine_sin,
            )
            for kind in range(2):
                high, low = split(pair[kind])
                tables[kind, j, 16 * a : 16 * a + 16, :] = high
                tables[kind, j, HALF + 16 * a : HALF + 16 * a + 16, :] = low

    each(0, BLOCKS, fill)
    even[HALF:TILE, HALF:TILE] = jnp.zeros((HALF, HALF), bf16)
    odd[HALF:TILE, HALF:TILE] = jnp.zeros((HALF, HALF), bf16)

    def load_lines(left, right):
        backward = (HALF - 1) - lax.broadcasted_iota(jnp.int32, (HALF, HALF), 1)
        left = jnp.take_along_axis(left, backward, axis=1)
        for ref, folded in ((even, right + left), (odd, right - left)):
            high, low = split(folded)
            ref[0:HALF, 0:HALF] = high
            ref[0:HALF, HALF:TILE] = high
            ref[HALF:TILE, 0:HALF] = low

    def load_chunks(x):
        x = x.reshape(BLOCKS * SHARE, TILE)
        load_lines(x[:, 0:HALF], x[:, HALF:TILE])

    def transform(j, cosine):
        by_sin = jnp.dot(odd[...], tables[0, j], preferred_element_type=f32)
        by_cos = jnp.dot(even[...], tables[1, j], preferred_element_type=f32)
        by_sin = by_sin[0:HALF] + by_sin[HALF:TILE]
        by_cos = by_cos[0:HALF] + by_cos[HALF:TILE]
        result = None
        for chunk in range(BLOCKS):
            rows = slice(SHARE * chunk, SHARE * chunk + SHARE)
            centre_sin = base_ref[j, CENTRE_SIN + chunk : CENTRE_SIN + chunk + 1, :]
            centre_cos = base_ref[j, CENTRE_COS + chunk : CENTRE_COS + chunk + 1, :]
            if cosine:
                term = centre_cos * by_cos[rows] - centre_sin * by_sin[rows]
            else:
                term = centre_sin * by_cos[rows] + centre_cos * by_sin[rows]
            result = term if result is None else result + term
        return result

    all_of(EX_A).wait_recv()
    load_chunks(charge_in[0:BLOCKS] + charge_in[BLOCKS : 2 * BLOCKS])
    for j in range(BLOCKS):
        modes = transform(j, False)
        modes_out[2 * j] = modes[:, 0:HALF]
        modes_out[2 * j + 1] = modes[:, HALF:TILE]
    for peer in plane_others:
        to_b(peer).start()
    modes_in[here] = modes_out[here]

    first_mode = here * HALF + ty * SHARE
    lane = lax.broadcasted_iota(jnp.int32, (SHARE, TILE), 1)
    sublane = lax.broadcasted_iota(jnp.int32, (SHARE, TILE), 0)
    mine = lane == sublane + lax.rem(first_mode, TILE)
    my_block = lax.div(first_mode, TILE)

    def of_mine(row):
        values = base_ref[my_block, row : row + 1, :]
        return jnp.sum(jnp.where(mine, values, f32(0)), axis=1, keepdims=True)

    my_eigen, my_wave = of_mine(EIGEN), of_mine(WAVE)

    all_of(EX_B).wait_recv()
    turned_out[...] = modes_in[...].reshape(TILE, HALF).T.reshape(RING, SHARE, TILE)
    for peer in ring_others:
        to_z(peer).start()
    spectrum_in[ty] = turned_out[ty]

    all_of(EX_Z).wait_recv()
    load_chunks(spectrum_in[...])
    scale = f32((2.0 / (GRID + 1)) ** 2)
    for j in range(BLOCKS):
        potential = transform(j, False) * scale / (my_eigen + base_ref[j, EIGEN : EIGEN + 1, :])
        scaled[0, j] = -my_wave * potential
        scaled[1, j] = -base_ref[j, WAVE : WAVE + 1, :] * potential

    for comp in range(2):
        load_chunks(scaled[comp])
        for j in range(BLOCKS):
            column_out[comp, j] = transform(j, comp == 1)
        for peer in ring_others:
            to_c(comp, peer).start()
        column_in[comp, ty] = column_out[comp, ty]

    wide = min(ONE_HOT_STEP, count)

    def one_hots(i):
        part = pl.ds(pl.multiple_of(i * wide, wide), wide)
        cells = lax.broadcasted_iota(jnp.int32, (TILE, wide), 0).astype(f32).astype(bf16)
        rows_two[:, part] = jnp.where(
            cells == row_two[:, part].astype(f32).astype(bf16), bf16(1), bf16(0)
        )

    @pl.when(beam == 1)
    def _():
        for item in cells_over:
            item.wait_recv()
        each(0, count // wide, one_hots)

    for comp in range(2):
        all_of(EX_C, comp).wait_recv()
        back_out[comp] = column_in[comp].reshape(HALF, TILE).T.reshape(PLANE, SHARE, HALF)
        for peer in plane_others:
            to_p(comp, peer).start()
        back_in[comp, here] = back_out[comp, here]

    for comp in range(2):
        all_of(EX_P, comp).wait_recv()
        load_lines(
            jnp.concatenate([back_in[comp, 2 * j] for j in range(BLOCKS)], axis=0),
            jnp.concatenate([back_in[comp, 2 * j + 1] for j in range(BLOCKS)], axis=0),
        )
        for j in range(BLOCKS):
            field_out[comp, j] = transform(j, comp == 0)
        if comp == 0:
            for peer in plane_all:
                to_dx(peer).start()
        else:
            for peer in plane_others:
                to_dy(peer).start()

    @pl.when(beam == 0)
    def _():
        to_dy(here).start()

    @pl.when(beam == 1)
    def _():
        field_in[2, here] = field_out[1, tx]

    loads[4].wait()
    turn = min(SAMPLE_STEP, count)

    def sample(slot, on_rows, cols, store):
        field = field_in[slot].reshape(TILE, TILE)
        field = 0.75 * field + 0.25 * pltpu.roll(field, TILE - 1, 1)
        field = kick_gain * (0.625 * field + 0.375 * pltpu.roll(field, TILE - 1, 0))
        high, low = split(field)
        parts[0:TILE, :] = high
        parts[TILE : 2 * TILE, :] = low

        def body(i):
            part = pl.ds(pl.multiple_of(i * turn, turn), turn)
            cells = lax.broadcasted_iota(jnp.int32, (TILE, turn), 0)
            near = jnp.dot(parts[...], on_rows[:, part], preferred_element_type=f32)
            near = near[0:TILE] + near[TILE : 2 * TILE]
            store(
                part,
                jnp.sum(jnp.where(cells == cols[:, part], near, f32(0)), axis=0, keepdims=True),
            )

        each(0, count // turn, body)

    def own(comp):
        def store(part, kick):
            out_ref[comp : comp + 1, part] = momenta_ref[comp : comp + 1, part] + kick

        return store

    def for_partner(part, kick):
        kicks_two[:, part] = kick

    all_of(EX_D).wait_recv()
    sample(0, on_rows, col_ref, own(0))

    @pl.when(beam == 1)
    def _():
        all_of(EX_D, 2).wait_recv()
        sample(2, rows_two, col_two, for_partner)
        kicks_back.start()
        all_of(EX_D, 1).wait_recv()
        sample(1, on_rows, col_ref, own(1))
        kicks_back.wait_send()
        all_of(EX_D, 2).wait_send()

    @pl.when(beam == 0)
    def _():
        kicks_back.wait_recv()
        out_ref[1:2, :] = momenta_ref[1:2, :] + kicks_in[...]
        for item in cells_over:
            item.wait_send()
        all_of(EX_D, 1).wait_send()

    for exchange in (EX_A, EX_B, EX_Z, EX_D):
        all_of(exchange).wait_send()
    for comp in range(2):
        for exchange in (EX_C, EX_P):
            all_of(exchange, comp).wait_send()


def shards(cell_row, cell_col, weights, momenta):
    count = cell_row.shape[1]
    dma = pltpu.SemaphoreType.DMA
    base = base_tables()
    kicked = pl.pallas_call(
        collide_kernel,
        out_shape=jax.ShapeDtypeStruct((2, count), f32),
        in_specs=[pl.BlockSpec(memory_space=pltpu.HBM)] * 5,
        out_specs=pl.BlockSpec(memory_space=pltpu.VMEM),
        scratch_shapes=[
            pltpu.VMEM((1, count), jnp.int32),
            pltpu.VMEM((1, count), jnp.int32),
            pltpu.VMEM((1, count), f32),
            pltpu.VMEM((2, count), f32),
            pltpu.VMEM(base.shape, f32),
            pltpu.VMEM((1, count), jnp.int32),
            pltpu.VMEM((1, count), jnp.int32),
            pltpu.VMEM((1, count), f32),
            pltpu.VMEM((1, count), f32),
            pltpu.VMEM((TILE, count), bf16),
            pltpu.VMEM((TILE, count), bf16),
            pltpu.VMEM((2 * TILE, TILE), f32),
            pltpu.VMEM((PLANE, SHARE, TILE), f32),
            pltpu.VMEM((2, BLOCKS, TILE, TILE), bf16),
            pltpu.VMEM((TILE, TILE), bf16),
            pltpu.VMEM((TILE, TILE), bf16),
            pltpu.VMEM((PLANE, SHARE, TILE), f32),
            pltpu.VMEM((PLANE, SHARE, HALF), f32),
            pltpu.VMEM((PLANE, SHARE, HALF), f32),
            pltpu.VMEM((RING, SHARE, TILE), f32),
            pltpu.VMEM((RING, SHARE, TILE), f32),
            pltpu.VMEM((2, BLOCKS, SHARE, TILE), f32),
            pltpu.VMEM((2, RING, SHARE, TILE), f32),
            pltpu.VMEM((2, RING, SHARE, TILE), f32),
            pltpu.VMEM((2, PLANE, SHARE, HALF), f32),
            pltpu.VMEM((2, PLANE, SHARE, HALF), f32),
            pltpu.VMEM((2, BLOCKS, SHARE, TILE), f32),
            pltpu.VMEM((3, PLANE, SHARE, TILE), f32),
            pltpu.VMEM((2 * TILE, TILE), bf16),
            dma((5,)), dma((EXCHANGES,)), dma((EXCHANGES,)),
        ],
        compiler_params=pltpu.CompilerParams(
            vmem_limit_bytes=50 * 1024 * 1024, collective_id=0, has_side_effects=True
        ),
        name="collide",
    )(
        *[
            pltpu.with_memory_space_constraint(array, pltpu.HBM)
            for array in (cell_row, cell_col, weights, momenta[0], jnp.asarray(base))
        ]
    )
    return kicked[None]


def solution(mesh):
    placed = (
        P("beam", ("tx", "ty", "dom")),
        P("beam", ("tx", "ty", "dom")),
        P("beam", ("tx", "ty", "dom")),
        P("beam", None, ("tx", "ty", "dom")),
    )
    return jax.shard_map(
        shards,
        mesh=mesh,
        in_specs=placed,
        out_specs=P("beam", None, ("tx", "ty", "dom")),
        check_vma=False,
    )
```

```python
import jax
import jax.numpy as jnp
import numpy as np
from jax import lax
from jax.experimental import pallas as pl
from jax.experimental.pallas import tpu as pltpu
from jax.sharding import PartitionSpec as P

GRID = 2048
TILE = 256
BLOCKS = 8
SHARE = 16
PLANE = 16
RING = 8
HALF = 128
DEPOSIT_STEP = 8192
SAMPLE_STEP = 8192
kick_gain = 2.0
f32 = jnp.float32
bf16 = jnp.bfloat16

COARSE_SIN, COARSE_COS, FINE_SIN, FINE_COS, CENTRE_SIN, CENTRE_COS, EIGEN, WAVE = (
    0, 8, 16, 32, 48, 56, 64, 65,
)
BASE_ROWS = 72

EX_A, EX_B, EX_Z, EX_C, EX_P, EX_D, EXCHANGES = 0, 1, 2, 3, 5, 7, 9


def base_tables():
    points = GRID + 1
    wave = np.arange(1, GRID + 1, dtype=np.int64)

    def angles(doubled):
        doubled = np.asarray(doubled, dtype=np.int64)
        return np.pi * ((doubled[:, None] * wave[None, :]) % (4 * points)) / (2 * points)

    coarse = angles(32 * np.arange(8))
    fine = angles(2 * np.arange(16) + 1)
    centre = angles(2 * TILE * np.arange(BLOCKS) + TILE + 1)
    rows = np.zeros((BASE_ROWS, GRID))
    rows[0:64] = np.concatenate(
        [np.sin(coarse), np.cos(coarse), np.sin(fine), np.cos(fine), np.sin(centre), np.cos(centre)]
    )
    rows[EIGEN] = 4.0 * np.sin(np.pi * wave / (2 * points)) ** 2
    rows[WAVE] = np.pi * wave / points
    blocks = rows.reshape(BASE_ROWS, BLOCKS, TILE).transpose(1, 0, 2)
    return np.ascontiguousarray(blocks).astype(np.float32)


def split(x):
    high = x.astype(bf16)
    low = (x - high.astype(f32)).astype(bf16)
    return high, low


def collide_kernel(
    row_hbm, col_hbm, weight_hbm, momenta_hbm, base_hbm, out_ref,
    row_ref, col_ref, weight_ref, momenta_ref, base_ref,
    on_rows, total, tile_out, tables, even, odd, charge_in, modes_out, modes_in, turned_out,
    spectrum_in, scaled, column_out, column_in, back_out, back_in, field_out, field_in, parts,
    load, sent, came,
):
    beam, tx = lax.axis_index("beam"), lax.axis_index("tx")
    ty, dom = lax.axis_index("ty"), lax.axis_index("dom")
    here = tx * 2 + dom
    count = row_ref.shape[1]

    loads = [
        pltpu.make_async_copy(src, dst, load.at[i])
        for i, (src, dst) in enumerate(
            [
                (row_hbm, row_ref), (col_hbm, col_ref), (weight_hbm, weight_ref),
                (base_hbm, base_ref), (momenta_hbm, momenta_ref),
            ]
        )
    ]
    for item in loads:
        item.start()

    def each(first, last, act):
        def body(i, carry):
            act(i)
            return carry

        lax.fori_loop(first, last, body, 0)

    def plane_id(peer):
        return {"tx": lax.div(peer, 2), "dom": lax.rem(peer, 2)}

    def other_id(peer):
        return {"beam": 1 - beam, "ty": peer}

    def ring_id(peer):
        return {"ty": peer}

    def hops(distance, size):
        return min(distance, size - distance)

    steps = [(dy, dx) for dy in range(4) for dx in range(4)]
    steps.sort(key=lambda step: -hops(step[0], 4) - hops(step[1], 4))
    plane_others = [
        lax.rem(lax.div(here, 4) + dy, 4) * 4 + lax.rem(lax.rem(here, 4) + dx, 4)
        for dy, dx in steps[:-1]
    ]
    ring_all = [
        lax.rem(ty + step, RING)
        for step in sorted(range(RING), key=lambda step: -hops(step, RING))
    ]
    ring_others = ring_all[:-1]

    def copy(src, dst, exchange, device):
        return pltpu.make_async_remote_copy(
            src_ref=src, dst_ref=dst, send_sem=sent.at[exchange], recv_sem=came.at[exchange],
            device_id=device, device_id_type=pl.DeviceIdType.MESH,
        )

    mine_in = dom * BLOCKS + tx

    def to_a(peer):
        return copy(tile_out.at[peer], charge_in.at[mine_in], EX_A, plane_id(peer))

    def to_b(peer):
        return copy(modes_out.at[peer], modes_in.at[here], EX_B, plane_id(peer))

    def to_z(peer):
        return copy(turned_out.at[peer], spectrum_in.at[ty], EX_Z, other_id(peer))

    def to_c(comp, peer):
        return copy(
            column_out.at[comp, peer], column_in.at[comp, ty], EX_C + comp, ring_id(peer)
        )

    def to_p(comp, peer):
        return copy(back_out.at[comp, peer], back_in.at[comp, here], EX_P + comp, plane_id(peer))

    def to_d(comp, peer):
        return copy(
            field_out.at[comp, lax.div(peer, 2)], field_in.at[comp, here],
            EX_D + comp, plane_id(peer),
        )

    others, rest = pl.ds(0, PLANE - 1), pl.ds(0, RING - 1)

    def all_of(exchange, comp=0):
        slots = {
            EX_A: charge_in.at[others],
            EX_B: modes_in.at[others],
            EX_Z: spectrum_in,
            EX_C: column_in.at[comp, rest],
            EX_P: back_in.at[comp, others],
            EX_D: field_in.at[comp, others],
        }[exchange]
        device = ring_id(ring_others[0]) if exchange in (EX_Z, EX_C) else plane_id(plane_others[0])
        return copy(slots, slots, exchange + comp, device)

    barrier = pltpu.get_barrier_semaphore()

    def greet(device):
        pl.semaphore_signal(
            barrier, inc=1, device_id=device, device_id_type=pl.DeviceIdType.MESH
        )

    for peer in ring_all:
        greet(other_id(peer))
    for peer in plane_others:
        greet(plane_id(peer))
    for peer in ring_others:
        greet(ring_id(peer))

    total[...] = jnp.zeros_like(total)
    for item in loads[0:3]:
        item.wait()
    step = min(DEPOSIT_STEP, count)

    def deposit(i):
        part = pl.ds(pl.multiple_of(i * step, step), step)
        cells = lax.broadcasted_iota(jnp.int32, (TILE, step), 0).astype(f32).astype(bf16)
        high, low = split(weight_ref[:, part])
        on_row = jnp.where(
            cells == row_ref[:, part].astype(f32).astype(bf16), bf16(1), bf16(0)
        )
        on_rows[:, part] = on_row
        hit = cells == col_ref[:, part].astype(f32).astype(bf16)
        on_col = jnp.concatenate(
            [jnp.where(hit, high, bf16(0)), jnp.where(hit, low, bf16(0))], axis=0
        )
        total[...] += lax.dot_general(
            on_col, on_row, (((1,), (1,)), ((), ())), preferred_element_type=f32
        )

    each(0, count // step, deposit)
    tile = total[0:TILE, :] + total[TILE : 2 * TILE, :]
    tile = 0.75 * tile + 0.25 * pltpu.roll(tile, 1, 1)
    tile = 0.625 * tile + 0.375 * pltpu.roll(tile, 1, 0)
    tile_out[...] = tile.reshape(PLANE, SHARE, TILE)

    pl.semaphore_wait(barrier, PLANE - 1 + RING + RING - 1)
    for peer in plane_others:
        to_a(peer).start()
    charge_in[mine_in] = tile_out[here]

    loads[3].wait()

    def fill(j):
        fine_sin = base_ref[j, FINE_SIN : FINE_SIN + 16, :]
        fine_cos = base_ref[j, FINE_COS : FINE_COS + 16, :]
        for a in range(8):
            coarse_sin = base_ref[j, COARSE_SIN + a : COARSE_SIN + a + 1, :]
            coarse_cos = base_ref[j, COARSE_COS + a : COARSE_COS + a + 1, :]
            pair = (
                coarse_sin * fine_cos + coarse_cos * fine_sin,
                coarse_cos * fine_cos - coarse_sin * fine_sin,
            )
            for kind in range(2):
                high, low = split(pair[kind])
                tables[kind, j, 16 * a : 16 * a + 16, :] = high
                tables[kind, j, HALF + 16 * a : HALF + 16 * a + 16, :] = low

    each(0, BLOCKS, fill)
    even[HALF:TILE, HALF:TILE] = jnp.zeros((HALF, HALF), bf16)
    odd[HALF:TILE, HALF:TILE] = jnp.zeros((HALF, HALF), bf16)

    def load_lines(left, right):
        backward = (HALF - 1) - lax.broadcasted_iota(jnp.int32, (HALF, HALF), 1)
        left = jnp.take_along_axis(left, backward, axis=1)
        for ref, folded in ((even, right + left), (odd, right - left)):
            high, low = split(folded)
            ref[0:HALF, 0:HALF] = high
            ref[0:HALF, HALF:TILE] = high
            ref[HALF:TILE, 0:HALF] = low

    def load_chunks(x):
        x = x.reshape(BLOCKS * SHARE, TILE)
        load_lines(x[:, 0:HALF], x[:, HALF:TILE])

    def transform(j, cosine):
        by_sin = jnp.dot(odd[...], tables[0, j], preferred_element_type=f32)
        by_cos = jnp.dot(even[...], tables[1, j], preferred_element_type=f32)
        by_sin = by_sin[0:HALF] + by_sin[HALF:TILE]
        by_cos = by_cos[0:HALF] + by_cos[HALF:TILE]
        result = None
        for chunk in range(BLOCKS):
            rows = slice(SHARE * chunk, SHARE * chunk + SHARE)
            centre_sin = base_ref[j, CENTRE_SIN + chunk : CENTRE_SIN + chunk + 1, :]
            centre_cos = base_ref[j, CENTRE_COS + chunk : CENTRE_COS + chunk + 1, :]
            if cosine:
                term = centre_cos * by_cos[rows] - centre_sin * by_sin[rows]
            else:
                term = centre_sin * by_cos[rows] + centre_cos * by_sin[rows]
            result = term if result is None else result + term
        return result

    all_of(EX_A).wait_recv()
    load_chunks(charge_in[0:BLOCKS] + charge_in[BLOCKS : 2 * BLOCKS])
    for j in range(BLOCKS):
        modes = transform(j, False)
        modes_out[2 * j] = modes[:, 0:HALF]
        modes_out[2 * j + 1] = modes[:, HALF:TILE]
    for peer in plane_others:
        to_b(peer).start()
    modes_in[here] = modes_out[here]

    first_mode = here * HALF + ty * SHARE
    lane = lax.broadcasted_iota(jnp.int32, (SHARE, TILE), 1)
    sublane = lax.broadcasted_iota(jnp.int32, (SHARE, TILE), 0)
    mine = lane == sublane + lax.rem(first_mode, TILE)
    my_block = lax.div(first_mode, TILE)

    def of_mine(row):
        values = base_ref[my_block, row : row + 1, :]
        return jnp.sum(jnp.where(mine, values, f32(0)), axis=1, keepdims=True)

    my_eigen, my_wave = of_mine(EIGEN), of_mine(WAVE)

    all_of(EX_B).wait_recv()
    turned_out[...] = modes_in[...].reshape(TILE, HALF).T.reshape(RING, SHARE, TILE)
    for peer in ring_all:
        to_z(peer).start()

    all_of(EX_Z).wait_recv()
    load_chunks(spectrum_in[...])
    scale = f32((2.0 / (GRID + 1)) ** 2)
    for j in range(BLOCKS):
        potential = transform(j, False) * scale / (my_eigen + base_ref[j, EIGEN : EIGEN + 1, :])
        scaled[0, j] = -my_wave * potential
        scaled[1, j] = -base_ref[j, WAVE : WAVE + 1, :] * potential

    for comp in range(2):
        load_chunks(scaled[comp])
        for j in range(BLOCKS):
            column_out[comp, j] = transform(j, comp == 1)
        for peer in ring_others:
            to_c(comp, peer).start()
        column_in[comp, ty] = column_out[comp, ty]

    for comp in range(2):
        all_of(EX_C, comp).wait_recv()
        back_out[comp] = column_in[comp].reshape(HALF, TILE).T.reshape(PLANE, SHARE, HALF)
        for peer in plane_others:
            to_p(comp, peer).start()
        back_in[comp, here] = back_out[comp, here]

    for comp in range(2):
        all_of(EX_P, comp).wait_recv()
        load_lines(
            jnp.concatenate([back_in[comp, 2 * j] for j in range(BLOCKS)], axis=0),
            jnp.concatenate([back_in[comp, 2 * j + 1] for j in range(BLOCKS)], axis=0),
        )
        for j in range(BLOCKS):
            field_out[comp, j] = transform(j, comp == 0)
        for peer in plane_others:
            to_d(comp, peer).start()
        field_in[comp, here] = field_out[comp, tx]

    loads[4].wait()
    turn = min(SAMPLE_STEP, count)
    for comp in range(2):
        all_of(EX_D, comp).wait_recv()
        field = field_in[comp].reshape(TILE, TILE)
        field = 0.75 * field + 0.25 * pltpu.roll(field, TILE - 1, 1)
        field = kick_gain * (0.625 * field + 0.375 * pltpu.roll(field, TILE - 1, 0))
        high, low = split(field)
        parts[0:TILE, :] = high
        parts[TILE : 2 * TILE, :] = low

        def sample(i, comp=comp):
            part = pl.ds(pl.multiple_of(i * turn, turn), turn)
            cells = lax.broadcasted_iota(jnp.int32, (TILE, turn), 0)
            near = jnp.dot(parts[...], on_rows[:, part], preferred_element_type=f32)
            near = near[0:TILE] + near[TILE : 2 * TILE]
            kick = jnp.sum(
                jnp.where(cells == col_ref[:, part], near, f32(0)), axis=0, keepdims=True
            )
            out_ref[comp : comp + 1, part] = momenta_ref[comp : comp + 1, part] + kick

        each(0, count // turn, sample)

    for exchange in (EX_A, EX_B, EX_Z):
        all_of(exchange).wait_send()
    for comp in range(2):
        for exchange in (EX_C, EX_P, EX_D):
            all_of(exchange, comp).wait_send()


def shards(cell_row, cell_col, weights, momenta):
    count = cell_row.shape[1]
    dma = pltpu.SemaphoreType.DMA
    base = base_tables()
    kicked = pl.pallas_call(
        collide_kernel,
        out_shape=jax.ShapeDtypeStruct((2, count), f32),
        in_specs=[pl.BlockSpec(memory_space=pltpu.HBM)] * 5,
        out_specs=pl.BlockSpec(memory_space=pltpu.VMEM),
        scratch_shapes=[
            pltpu.VMEM((1, count), jnp.int32),
            pltpu.VMEM((1, count), jnp.int32),
            pltpu.VMEM((1, count), f32),
            pltpu.VMEM((2, count), f32),
            pltpu.VMEM(base.shape, f32),
            pltpu.VMEM((TILE, count), bf16),
            pltpu.VMEM((2 * TILE, TILE), f32),
            pltpu.VMEM((PLANE, SHARE, TILE), f32),
            pltpu.VMEM((2, BLOCKS, TILE, TILE), bf16),
            pltpu.VMEM((TILE, TILE), bf16),
            pltpu.VMEM((TILE, TILE), bf16),
            pltpu.VMEM((PLANE, SHARE, TILE), f32),
            pltpu.VMEM((PLANE, SHARE, HALF), f32),
            pltpu.VMEM((PLANE, SHARE, HALF), f32),
            pltpu.VMEM((RING, SHARE, TILE), f32),
            pltpu.VMEM((RING, SHARE, TILE), f32),
            pltpu.VMEM((2, BLOCKS, SHARE, TILE), f32),
            pltpu.VMEM((2, RING, SHARE, TILE), f32),
            pltpu.VMEM((2, RING, SHARE, TILE), f32),
            pltpu.VMEM((2, PLANE, SHARE, HALF), f32),
            pltpu.VMEM((2, PLANE, SHARE, HALF), f32),
            pltpu.VMEM((2, BLOCKS, SHARE, TILE), f32),
            pltpu.VMEM((2, PLANE, SHARE, TILE), f32),
            pltpu.VMEM((2 * TILE, TILE), bf16),
            dma((5,)), dma((EXCHANGES,)), dma((EXCHANGES,)),
        ],
        compiler_params=pltpu.CompilerParams(
            vmem_limit_bytes=48 * 1024 * 1024, collective_id=0, has_side_effects=True
        ),
        name="collide",
    )(
        *[
            pltpu.with_memory_space_constraint(array, pltpu.HBM)
            for array in (cell_row, cell_col, weights, momenta[0], jnp.asarray(base))
        ]
    )
    return kicked[None]


def solution(mesh):
    placed = (
        P("beam", ("tx", "ty", "dom")),
        P("beam", ("tx", "ty", "dom")),
        P("beam", ("tx", "ty", "dom")),
        P("beam", None, ("tx", "ty", "dom")),
    )
    return jax.shard_map(
        shards,
        mesh=mesh,
        in_specs=placed,
        out_specs=P("beam", None, ("tx", "ty", "dom")),
        check_vma=False,
    )
```

```python
import jax
import jax.numpy as jnp
import numpy as np
from jax import lax
from jax.experimental import pallas as pl
from jax.experimental.pallas import tpu as pltpu
from jax.sharding import PartitionSpec as P

GRID = 2048
TILE = 256
BLOCKS = 8
SHARE = 16
PLANE = 16
RING = 8
HALF = 128
DEPOSIT_STEP = 16384
SAMPLE_STEP = 8192
kick_gain = 2.0
f32 = jnp.float32
bf16 = jnp.bfloat16

COARSE_SIN, COARSE_COS, FINE_SIN, FINE_COS, CENTRE_SIN, CENTRE_COS, EIGEN, WAVE = (
    0, 8, 16, 32, 48, 56, 64, 65,
)
BASE_ROWS = 72

EX_A, EX_B, EX_Z, EX_C, EX_P, EX_D, EXCHANGES = 0, 1, 2, 3, 5, 7, 9


def base_tables():
    points = GRID + 1
    wave = np.arange(1, GRID + 1, dtype=np.int64)

    def angles(doubled):
        doubled = np.asarray(doubled, dtype=np.int64)
        return np.pi * ((doubled[:, None] * wave[None, :]) % (4 * points)) / (2 * points)

    coarse = angles(32 * np.arange(8))
    fine = angles(2 * np.arange(16) + 1)
    centre = angles(2 * TILE * np.arange(BLOCKS) + TILE + 1)
    rows = np.zeros((BASE_ROWS, GRID))
    rows[0:64] = np.concatenate(
        [np.sin(coarse), np.cos(coarse), np.sin(fine), np.cos(fine), np.sin(centre), np.cos(centre)]
    )
    rows[EIGEN] = 4.0 * np.sin(np.pi * wave / (2 * points)) ** 2
    rows[WAVE] = np.pi * wave / points
    blocks = rows.reshape(BASE_ROWS, BLOCKS, TILE).transpose(1, 0, 2)
    return np.ascontiguousarray(blocks).astype(np.float32)


def split(x):
    high = x.astype(bf16)
    low = (x - high.astype(f32)).astype(bf16)
    return high, low


def collide_kernel(
    row_hbm, col_hbm, weight_hbm, momenta_hbm, base_hbm, out_ref,
    row_ref, col_ref, weight_ref, momenta_ref, base_ref,
    on_rows, total, tile_out, tables, even, odd, charge_in, modes_out, modes_in, turned_out,
    spectrum_in, scaled, column_out, column_in, back_out, back_in, field_out, field_in, parts,
    load, sent, came,
):
    beam, tx = lax.axis_index("beam"), lax.axis_index("tx")
    ty, dom = lax.axis_index("ty"), lax.axis_index("dom")
    here = tx * 2 + dom
    count = row_ref.shape[1]

    loads = [
        pltpu.make_async_copy(src, dst, load.at[i])
        for i, (src, dst) in enumerate(
            [
                (row_hbm, row_ref), (col_hbm, col_ref), (weight_hbm, weight_ref),
                (base_hbm, base_ref), (momenta_hbm, momenta_ref),
            ]
        )
    ]
    for item in loads:
        item.start()

    def each(first, last, act):
        def body(i, carry):
            act(i)
            return carry

        lax.fori_loop(first, last, body, 0)

    def plane_id(peer):
        return {"tx": lax.div(peer, 2), "dom": lax.rem(peer, 2)}

    def other_id(peer):
        return {"beam": 1 - beam, "tx": lax.div(peer, 2), "dom": lax.rem(peer, 2)}

    def ring_id(peer):
        return {"ty": peer}

    def hops(distance, size):
        return min(distance, size - distance)

    steps = [(dy, dx) for dy in range(4) for dx in range(4)]
    steps.sort(key=lambda step: -hops(step[0], 4) - hops(step[1], 4))
    plane_all = [
        lax.rem(lax.div(here, 4) + dy, 4) * 4 + lax.rem(lax.rem(here, 4) + dx, 4)
        for dy, dx in steps
    ]
    plane_others = plane_all[:-1]
    ring_others = [
        lax.rem(ty + step, RING)
        for step in sorted(range(1, RING), key=lambda step: -hops(step, RING))
    ]

    def copy(src, dst, exchange, device):
        return pltpu.make_async_remote_copy(
            src_ref=src, dst_ref=dst, send_sem=sent.at[exchange], recv_sem=came.at[exchange],
            device_id=device, device_id_type=pl.DeviceIdType.MESH,
        )

    mine_in = dom * BLOCKS + tx

    def to_a(peer):
        return copy(tile_out.at[peer], charge_in.at[mine_in], EX_A, plane_id(peer))

    def to_b(peer):
        return copy(modes_out.at[peer], modes_in.at[here], EX_B, other_id(peer))

    def to_z(peer):
        return copy(turned_out.at[peer], spectrum_in.at[ty], EX_Z, ring_id(peer))

    def to_c(comp, peer):
        return copy(
            column_out.at[comp, peer], column_in.at[comp, ty], EX_C + comp, ring_id(peer)
        )

    def to_p(comp, peer):
        return copy(back_out.at[comp, peer], back_in.at[comp, here], EX_P + comp, plane_id(peer))

    def to_d(comp, peer):
        return copy(
            field_out.at[comp, lax.div(peer, 2)], field_in.at[comp, here],
            EX_D + comp, plane_id(peer),
        )

    others, rest = pl.ds(0, PLANE - 1), pl.ds(0, RING - 1)

    def all_of(exchange, comp=0):
        slots = {
            EX_A: charge_in.at[others],
            EX_B: modes_in,
            EX_Z: spectrum_in.at[rest],
            EX_C: column_in.at[comp, rest],
            EX_P: back_in.at[comp, others],
            EX_D: field_in.at[comp, others],
        }[exchange]
        device = ring_id(ring_others[0]) if exchange in (EX_Z, EX_C) else plane_id(plane_others[0])
        return copy(slots, slots, exchange + comp, device)

    barrier = pltpu.get_barrier_semaphore()

    def greet(device):
        pl.semaphore_signal(
            barrier, inc=1, device_id=device, device_id_type=pl.DeviceIdType.MESH
        )

    for peer in plane_all:
        greet(other_id(peer))
    for peer in plane_others:
        greet(plane_id(peer))
    for peer in ring_others:
        greet(ring_id(peer))

    total[...] = jnp.zeros_like(total)
    for item in loads[0:3]:
        item.wait()
    step = min(DEPOSIT_STEP, count)

    def deposit(i):
        part = pl.ds(pl.multiple_of(i * step, step), step)
        cells = lax.broadcasted_iota(jnp.int32, (TILE, step), 0).astype(f32).astype(bf16)
        high, low = split(weight_ref[:, part])
        on_row = jnp.where(
            cells == row_ref[:, part].astype(f32).astype(bf16), bf16(1), bf16(0)
        )
        on_rows[:, part] = on_row
        hit = cells == col_ref[:, part].astype(f32).astype(bf16)
        on_col = jnp.concatenate(
            [jnp.where(hit, high, bf16(0)), jnp.where(hit, low, bf16(0))], axis=0
        )
        total[...] += lax.dot_general(
            on_col, on_row, (((1,), (1,)), ((), ())), preferred_element_type=f32
        )

    each(0, count // step, deposit)
    tile = total[0:TILE, :] + total[TILE : 2 * TILE, :]
    tile = 0.75 * tile + 0.25 * pltpu.roll(tile, 1, 1)
    tile = 0.625 * tile + 0.375 * pltpu.roll(tile, 1, 0)
    tile_out[...] = tile.reshape(PLANE, SHARE, TILE)

    pl.semaphore_wait(barrier, PLANE + PLANE - 1 + RING - 1)
    for peer in plane_others:
        to_a(peer).start()
    charge_in[mine_in] = tile_out[here]

    loads[3].wait()

    def fill(j):
        fine_sin = base_ref[j, FINE_SIN : FINE_SIN + 16, :]
        fine_cos = base_ref[j, FINE_COS : FINE_COS + 16, :]
        for a in range(8):
            coarse_sin = base_ref[j, COARSE_SIN + a : COARSE_SIN + a + 1, :]
            coarse_cos = base_ref[j, COARSE_COS + a : COARSE_COS + a + 1, :]
            pair = (
                coarse_sin * fine_cos + coarse_cos * fine_sin,
                coarse_cos * fine_cos - coarse_sin * fine_sin,
            )
            for kind in range(2):
                high, low = split(pair[kind])
                tables[kind, j, 16 * a : 16 * a + 16, :] = high
                tables[kind, j, HALF + 16 * a : HALF + 16 * a + 16, :] = low

    each(0, BLOCKS, fill)
    even[HALF:TILE, HALF:TILE] = jnp.zeros((HALF, HALF), bf16)
    odd[HALF:TILE, HALF:TILE] = jnp.zeros((HALF, HALF), bf16)

    def load_lines(left, right):
        backward = (HALF - 1) - lax.broadcasted_iota(jnp.int32, (HALF, HALF), 1)
        left = jnp.take_along_axis(left, backward, axis=1)
        for ref, folded in ((even, right + left), (odd, right - left)):
            high, low = split(folded)
            ref[0:HALF, 0:HALF] = high
            ref[0:HALF, HALF:TILE] = high
            ref[HALF:TILE, 0:HALF] = low

    def load_chunks(x):
        x = x.reshape(BLOCKS * SHARE, TILE)
        load_lines(x[:, 0:HALF], x[:, HALF:TILE])

    def transform(j, cosine):
        by_sin = jnp.dot(odd[...], tables[0, j], preferred_element_type=f32)
        by_cos = jnp.dot(even[...], tables[1, j], preferred_element_type=f32)
        by_sin = by_sin[0:HALF] + by_sin[HALF:TILE]
        by_cos = by_cos[0:HALF] + by_cos[HALF:TILE]
        result = None
        for chunk in range(BLOCKS):
            rows = slice(SHARE * chunk, SHARE * chunk + SHARE)
            centre_sin = base_ref[j, CENTRE_SIN + chunk : CENTRE_SIN + chunk + 1, :]
            centre_cos = base_ref[j, CENTRE_COS + chunk : CENTRE_COS + chunk + 1, :]
            if cosine:
                term = centre_cos * by_cos[rows] - centre_sin * by_sin[rows]
            else:
                term = centre_sin * by_cos[rows] + centre_cos * by_sin[rows]
            result = term if result is None else result + term
        return result

    all_of(EX_A).wait_recv()
    load_chunks(charge_in[0:BLOCKS] + charge_in[BLOCKS : 2 * BLOCKS])
    for j in range(BLOCKS):
        modes = transform(j, False)
        modes_out[2 * j] = modes[:, 0:HALF]
        modes_out[2 * j + 1] = modes[:, HALF:TILE]
    for peer in plane_all:
        to_b(peer).start()

    first_mode = here * HALF + ty * SHARE
    lane = lax.broadcasted_iota(jnp.int32, (SHARE, TILE), 1)
    sublane = lax.broadcasted_iota(jnp.int32, (SHARE, TILE), 0)
    mine = lane == sublane + lax.rem(first_mode, TILE)
    my_block = lax.div(first_mode, TILE)

    def of_mine(row):
        values = base_ref[my_block, row : row + 1, :]
        return jnp.sum(jnp.where(mine, values, f32(0)), axis=1, keepdims=True)

    my_eigen, my_wave = of_mine(EIGEN), of_mine(WAVE)

    all_of(EX_B).wait_recv()
    turned_out[...] = modes_in[...].reshape(TILE, HALF).T.reshape(RING, SHARE, TILE)
    for peer in ring_others:
        to_z(peer).start()
    spectrum_in[ty] = turned_out[ty]

    all_of(EX_Z).wait_recv()
    load_chunks(spectrum_in[...])
    scale = f32((2.0 / (GRID + 1)) ** 2)
    for j in range(BLOCKS):
        potential = transform(j, False) * scale / (my_eigen + base_ref[j, EIGEN : EIGEN + 1, :])
        scaled[0, j] = -my_wave * potential
        scaled[1, j] = -base_ref[j, WAVE : WAVE + 1, :] * potential

    for comp in range(2):
        load_chunks(scaled[comp])
        for j in range(BLOCKS):
            column_out[comp, j] = transform(j, comp == 1)
        for peer in ring_others:
            to_c(comp, peer).start()
        column_in[comp, ty] = column_out[comp, ty]

    for comp in range(2):
        all_of(EX_C, comp).wait_recv()
        back_out[comp] = column_in[comp].reshape(HALF, TILE).T.reshape(PLANE, SHARE, HALF)
        for peer in plane_others:
            to_p(comp, peer).start()
        back_in[comp, here] = back_out[comp, here]

    for comp in range(2):
        all_of(EX_P, comp).wait_recv()
        load_lines(
            jnp.concatenate([back_in[comp, 2 * j] for j in range(BLOCKS)], axis=0),
            jnp.concatenate([back_in[comp, 2 * j + 1] for j in range(BLOCKS)], axis=0),
        )
        for j in range(BLOCKS):
            field_out[comp, j] = transform(j, comp == 0)
        for peer in plane_others:
            to_d(comp, peer).start()
        field_in[comp, here] = field_out[comp, tx]

    loads[4].wait()
    turn = min(SAMPLE_STEP, count)
    for comp in range(2):
        all_of(EX_D, comp).wait_recv()
        field = field_in[comp].reshape(TILE, TILE)
        field = 0.75 * field + 0.25 * pltpu.roll(field, TILE - 1, 1)
        field = kick_gain * (0.625 * field + 0.375 * pltpu.roll(field, TILE - 1, 0))
        high, low = split(field)
        parts[0:TILE, :] = high
        parts[TILE : 2 * TILE, :] = low

        def sample(i, comp=comp):
            part = pl.ds(pl.multiple_of(i * turn, turn), turn)
            cells = lax.broadcasted_iota(jnp.int32, (TILE, turn), 0)
            near = jnp.dot(parts[...], on_rows[:, part], preferred_element_type=f32)
            near = near[0:TILE] + near[TILE : 2 * TILE]
            kick = jnp.sum(
                jnp.where(cells == col_ref[:, part], near, f32(0)), axis=0, keepdims=True
            )
            out_ref[comp : comp + 1, part] = momenta_ref[comp : comp + 1, part] + kick

        each(0, count // turn, sample)

    for exchange in (EX_A, EX_B, EX_Z):
        all_of(exchange).wait_send()
    for comp in range(2):
        for exchange in (EX_C, EX_P, EX_D):
            all_of(exchange, comp).wait_send()


def shards(cell_row, cell_col, weights, momenta):
    count = cell_row.shape[1]
    dma = pltpu.SemaphoreType.DMA
    base = base_tables()
    kicked = pl.pallas_call(
        collide_kernel,
        out_shape=jax.ShapeDtypeStruct((2, count), f32),
        in_specs=[pl.BlockSpec(memory_space=pltpu.HBM)] * 5,
        out_specs=pl.BlockSpec(memory_space=pltpu.VMEM),
        scratch_shapes=[
            pltpu.VMEM((1, count), jnp.int32),
            pltpu.VMEM((1, count), jnp.int32),
            pltpu.VMEM((1, count), f32),
            pltpu.VMEM((2, count), f32),
            pltpu.VMEM(base.shape, f32),
            pltpu.VMEM((TILE, count), bf16),
            pltpu.VMEM((2 * TILE, TILE), f32),
            pltpu.VMEM((PLANE, SHARE, TILE), f32),
            pltpu.VMEM((2, BLOCKS, TILE, TILE), bf16),
            pltpu.VMEM((TILE, TILE), bf16),
            pltpu.VMEM((TILE, TILE), bf16),
            pltpu.VMEM((PLANE, SHARE, TILE), f32),
            pltpu.VMEM((PLANE, SHARE, HALF), f32),
            pltpu.VMEM((PLANE, SHARE, HALF), f32),
            pltpu.VMEM((RING, SHARE, TILE), f32),
            pltpu.VMEM((RING, SHARE, TILE), f32),
            pltpu.VMEM((2, BLOCKS, SHARE, TILE), f32),
            pltpu.VMEM((2, RING, SHARE, TILE), f32),
            pltpu.VMEM((2, RING, SHARE, TILE), f32),
            pltpu.VMEM((2, PLANE, SHARE, HALF), f32),
            pltpu.VMEM((2, PLANE, SHARE, HALF), f32),
            pltpu.VMEM((2, BLOCKS, SHARE, TILE), f32),
            pltpu.VMEM((2, PLANE, SHARE, TILE), f32),
            pltpu.VMEM((2 * TILE, TILE), bf16),
            dma((5,)), dma((EXCHANGES,)), dma((EXCHANGES,)),
        ],
        compiler_params=pltpu.CompilerParams(
            vmem_limit_bytes=48 * 1024 * 1024, collective_id=0, has_side_effects=True
        ),
        name="collide",
    )(
        *[
            pltpu.with_memory_space_constraint(array, pltpu.HBM)
            for array in (cell_row, cell_col, weights, momenta[0], jnp.asarray(base))
        ]
    )
    return kicked[None]


def solution(mesh):
    placed = (
        P("beam", ("tx", "ty", "dom")),
        P("beam", ("tx", "ty", "dom")),
        P("beam", ("tx", "ty", "dom")),
        P("beam", None, ("tx", "ty", "dom")),
    )
    return jax.shard_map(
        shards,
        mesh=mesh,
        in_specs=placed,
        out_specs=P("beam", None, ("tx", "ty", "dom")),
        check_vma=False,
    )
```

```python
import jax
import jax.numpy as jnp
import numpy as np
from jax import lax
from jax.experimental import pallas as pl
from jax.experimental.pallas import tpu as pltpu
from jax.sharding import PartitionSpec as P

GRID = 2048
TILE = 256
BLOCKS = 8
SHARE = 16
PLANE = 16
RING = 8
HALF = 128
DEPOSIT_STEP = 8192
SAMPLE_STEP = 8192
kick_gain = 2.0
f32 = jnp.float32
bf16 = jnp.bfloat16

COARSE_SIN, COARSE_COS, FINE_SIN, FINE_COS, CENTRE_SIN, CENTRE_COS, EIGEN, WAVE = (
    0, 8, 16, 32, 48, 56, 64, 65,
)
BASE_ROWS = 72

EX_A, EX_B, EX_Z, EX_C, EX_P, EX_D, EXCHANGES = 0, 1, 2, 3, 5, 7, 9


def base_tables():
    points = GRID + 1
    wave = np.arange(1, GRID + 1, dtype=np.int64)

    def angles(doubled):
        doubled = np.asarray(doubled, dtype=np.int64)
        return np.pi * ((doubled[:, None] * wave[None, :]) % (4 * points)) / (2 * points)

    coarse = angles(32 * np.arange(8))
    fine = angles(2 * np.arange(16) + 1)
    centre = angles(2 * TILE * np.arange(BLOCKS) + TILE + 1)
    rows = np.zeros((BASE_ROWS, GRID))
    rows[0:64] = np.concatenate(
        [np.sin(coarse), np.cos(coarse), np.sin(fine), np.cos(fine), np.sin(centre), np.cos(centre)]
    )
    rows[EIGEN] = 4.0 * np.sin(np.pi * wave / (2 * points)) ** 2
    rows[WAVE] = np.pi * wave / points
    blocks = rows.reshape(BASE_ROWS, BLOCKS, TILE).transpose(1, 0, 2)
    return np.ascontiguousarray(blocks).astype(np.float32)


def split(x):
    high = x.astype(bf16)
    low = (x - high.astype(f32)).astype(bf16)
    return high, low


def collide_kernel(
    row_hbm, col_hbm, weight_hbm, momenta_hbm, base_hbm, out_ref,
    row_ref, col_ref, weight_ref, momenta_ref, base_ref,
    on_rows, total, tile_out, tables, even, odd, charge_in, modes_out, modes_in, turned_out,
    spectrum_in, scaled, column_out, column_in, back_out, back_in, field_out, field_in, parts,
    load, sent, came,
):
    beam, tx = lax.axis_index("beam"), lax.axis_index("tx")
    ty, dom = lax.axis_index("ty"), lax.axis_index("dom")
    here = tx * 2 + dom
    count = row_ref.shape[1]

    loads = [
        pltpu.make_async_copy(src, dst, load.at[i])
        for i, (src, dst) in enumerate(
            [
                (row_hbm, row_ref), (col_hbm, col_ref), (weight_hbm, weight_ref),
                (base_hbm, base_ref), (momenta_hbm, momenta_ref),
            ]
        )
    ]
    for item in loads:
        item.start()

    def each(first, last, act):
        def body(i, carry):
            act(i)
            return carry

        lax.fori_loop(first, last, body, 0)

    def plane_id(peer):
        return {"tx": lax.div(peer, 2), "dom": lax.rem(peer, 2)}

    def other_id(peer):
        return {"beam": 1 - beam, "tx": lax.div(peer, 2), "dom": lax.rem(peer, 2)}

    def ring_id(peer):
        return {"ty": peer}

    def hops(distance, size):
        return min(distance, size - distance)

    steps = [(dy, dx) for dy in range(4) for dx in range(4)]
    steps.sort(key=lambda step: -hops(step[0], 4) - hops(step[1], 4))
    plane_all = [
        lax.rem(lax.div(here, 4) + dy, 4) * 4 + lax.rem(lax.rem(here, 4) + dx, 4)
        for dy, dx in steps
    ]
    plane_others = plane_all[:-1]
    ring_others = [
        lax.rem(ty + step, RING)
        for step in sorted(range(1, RING), key=lambda step: -hops(step, RING))
    ]

    def copy(src, dst, exchange, device):
        return pltpu.make_async_remote_copy(
            src_ref=src, dst_ref=dst, send_sem=sent.at[exchange], recv_sem=came.at[exchange],
            device_id=device, device_id_type=pl.DeviceIdType.MESH,
        )

    mine_in = dom * BLOCKS + tx

    def to_a(peer):
        return copy(tile_out.at[peer], charge_in.at[mine_in], EX_A, plane_id(peer))

    def to_b(peer):
        return copy(modes_out.at[peer], modes_in.at[here], EX_B, other_id(peer))

    def to_z(peer):
        return copy(turned_out.at[peer], spectrum_in.at[ty], EX_Z, ring_id(peer))

    def to_c(comp, peer):
        return copy(
            column_out.at[comp, peer], column_in.at[comp, ty], EX_C + comp, ring_id(peer)
        )

    def to_p(comp, peer):
        return copy(back_out.at[comp, peer], back_in.at[comp, here], EX_P + comp, plane_id(peer))

    def to_d(comp, peer):
        return copy(
            field_out.at[comp, lax.div(peer, 2)], field_in.at[comp, here],
            EX_D + comp, plane_id(peer),
        )

    others, rest = pl.ds(0, PLANE - 1), pl.ds(0, RING - 1)

    def all_of(exchange, comp=0):
        slots = {
            EX_A: charge_in.at[others],
            EX_B: modes_in,
            EX_Z: spectrum_in.at[rest],
            EX_C: column_in.at[comp, rest],
            EX_P: back_in.at[comp, others],
            EX_D: field_in.at[comp, others],
        }[exchange]
        device = ring_id(ring_others[0]) if exchange in (EX_Z, EX_C) else plane_id(plane_others[0])
        return copy(slots, slots, exchange + comp, device)

    barrier = pltpu.get_barrier_semaphore()

    def greet(device):
        pl.semaphore_signal(
            barrier, inc=1, device_id=device, device_id_type=pl.DeviceIdType.MESH
        )

    for peer in plane_all:
        greet(other_id(peer))
    for peer in plane_others:
        greet(plane_id(peer))
    for peer in ring_others:
        greet(ring_id(peer))

    total[...] = jnp.zeros_like(total)
    for item in loads[0:3]:
        item.wait()
    step = min(DEPOSIT_STEP, count)

    def deposit(i):
        part = pl.ds(pl.multiple_of(i * step, step), step)
        cells = lax.broadcasted_iota(jnp.int32, (TILE, step), 0).astype(f32).astype(bf16)
        high, low = split(weight_ref[:, part])
        on_row = jnp.where(
            cells == row_ref[:, part].astype(f32).astype(bf16), bf16(1), bf16(0)
        )
        on_rows[:, part] = on_row
        hit = cells == col_ref[:, part].astype(f32).astype(bf16)
        on_col = jnp.concatenate(
            [jnp.where(hit, high, bf16(0)), jnp.where(hit, low, bf16(0))], axis=0
        )
        total[...] += lax.dot_general(
            on_col, on_row, (((1,), (1,)), ((), ())), preferred_element_type=f32
        )

    each(0, count // step, deposit)
    tile = total[0:TILE, :] + total[TILE : 2 * TILE, :]
    tile = 0.75 * tile + 0.25 * pltpu.roll(tile, 1, 1)
    tile = 0.625 * tile + 0.375 * pltpu.roll(tile, 1, 0)
    tile_out[...] = tile.reshape(PLANE, SHARE, TILE)

    pl.semaphore_wait(barrier, PLANE + PLANE - 1 + RING - 1)
    for peer in plane_others:
        to_a(peer).start()
    charge_in[mine_in] = tile_out[here]

    loads[3].wait()

    def fill(j):
        fine_sin = base_ref[j, FINE_SIN : FINE_SIN + 16, :]
        fine_cos = base_ref[j, FINE_COS : FINE_COS + 16, :]
        for a in range(8):
            coarse_sin = base_ref[j, COARSE_SIN + a : COARSE_SIN + a + 1, :]
            coarse_cos = base_ref[j, COARSE_COS + a : COARSE_COS + a + 1, :]
            pair = (
                coarse_sin * fine_cos + coarse_cos * fine_sin,
                coarse_cos * fine_cos - coarse_sin * fine_sin,
            )
            for kind in range(2):
                high, low = split(pair[kind])
                tables[kind, j, 16 * a : 16 * a + 16, :] = high
                tables[kind, j, HALF + 16 * a : HALF + 16 * a + 16, :] = low

    each(0, BLOCKS, fill)
    even[HALF:TILE, HALF:TILE] = jnp.zeros((HALF, HALF), bf16)
    odd[HALF:TILE, HALF:TILE] = jnp.zeros((HALF, HALF), bf16)

    def load_lines(left, right):
        backward = (HALF - 1) - lax.broadcasted_iota(jnp.int32, (HALF, HALF), 1)
        left = jnp.take_along_axis(left, backward, axis=1)
        for ref, folded in ((even, right + left), (odd, right - left)):
            high, low = split(folded)
            ref[0:HALF, 0:HALF] = high
            ref[0:HALF, HALF:TILE] = high
            ref[HALF:TILE, 0:HALF] = low

    def load_chunks(x):
        x = x.reshape(BLOCKS * SHARE, TILE)
        load_lines(x[:, 0:HALF], x[:, HALF:TILE])

    def transform(j, cosine):
        by_sin = jnp.dot(odd[...], tables[0, j], preferred_element_type=f32)
        by_cos = jnp.dot(even[...], tables[1, j], preferred_element_type=f32)
        by_sin = by_sin[0:HALF] + by_sin[HALF:TILE]
        by_cos = by_cos[0:HALF] + by_cos[HALF:TILE]
        result = None
        for chunk in range(BLOCKS):
            rows = slice(SHARE * chunk, SHARE * chunk + SHARE)
            centre_sin = base_ref[j, CENTRE_SIN + chunk : CENTRE_SIN + chunk + 1, :]
            centre_cos = base_ref[j, CENTRE_COS + chunk : CENTRE_COS + chunk + 1, :]
            if cosine:
                term = centre_cos * by_cos[rows] - centre_sin * by_sin[rows]
            else:
                term = centre_sin * by_cos[rows] + centre_cos * by_sin[rows]
            result = term if result is None else result + term
        return result

    all_of(EX_A).wait_recv()
    load_chunks(charge_in[0:BLOCKS] + charge_in[BLOCKS : 2 * BLOCKS])
    for j in range(BLOCKS):
        modes = transform(j, False)
        modes_out[2 * j] = modes[:, 0:HALF]
        modes_out[2 * j + 1] = modes[:, HALF:TILE]
    for peer in plane_all:
        to_b(peer).start()

    first_mode = here * HALF + ty * SHARE
    lane = lax.broadcasted_iota(jnp.int32, (SHARE, TILE), 1)
    sublane = lax.broadcasted_iota(jnp.int32, (SHARE, TILE), 0)
    mine = lane == sublane + lax.rem(first_mode, TILE)
    my_block = lax.div(first_mode, TILE)

    def of_mine(row):
        values = base_ref[my_block, row : row + 1, :]
        return jnp.sum(jnp.where(mine, values, f32(0)), axis=1, keepdims=True)

    my_eigen, my_wave = of_mine(EIGEN), of_mine(WAVE)

    all_of(EX_B).wait_recv()
    turned_out[...] = modes_in[...].reshape(TILE, HALF).T.reshape(RING, SHARE, TILE)
    for peer in ring_others:
        to_z(peer).start()
    spectrum_in[ty] = turned_out[ty]

    all_of(EX_Z).wait_recv()
    load_chunks(spectrum_in[...])
    scale = f32((2.0 / (GRID + 1)) ** 2)
    for j in range(BLOCKS):
        potential = transform(j, False) * scale / (my_eigen + base_ref[j, EIGEN : EIGEN + 1, :])
        scaled[0, j] = -my_wave * potential
        scaled[1, j] = -base_ref[j, WAVE : WAVE + 1, :] * potential

    for comp in range(2):
        load_chunks(scaled[comp])
        for j in range(BLOCKS):
            column_out[comp, j] = transform(j, comp == 1)
        for peer in ring_others:
            to_c(comp, peer).start()
        column_in[comp, ty] = column_out[comp, ty]

    for comp in range(2):
        all_of(EX_C, comp).wait_recv()
        back_out[comp] = column_in[comp].reshape(HALF, TILE).T.reshape(PLANE, SHARE, HALF)
        for peer in plane_others:
            to_p(comp, peer).start()
        back_in[comp, here] = back_out[comp, here]

    for comp in range(2):
        all_of(EX_P, comp).wait_recv()
        load_lines(
            jnp.concatenate([back_in[comp, 2 * j] for j in range(BLOCKS)], axis=0),
            jnp.concatenate([back_in[comp, 2 * j + 1] for j in range(BLOCKS)], axis=0),
        )
        for j in range(BLOCKS):
            field_out[comp, j] = transform(j, comp == 0)
        for peer in plane_others:
            to_d(comp, peer).start()
        field_in[comp, here] = field_out[comp, tx]

    loads[4].wait()
    turn = min(SAMPLE_STEP, count)
    for comp in range(2):
        all_of(EX_D, comp).wait_recv()
        field = field_in[comp].reshape(TILE, TILE)
        field = 0.75 * field + 0.25 * pltpu.roll(field, TILE - 1, 1)
        field = kick_gain * (0.625 * field + 0.375 * pltpu.roll(field, TILE - 1, 0))
        high, low = split(field)
        parts[0:TILE, :] = high
        parts[TILE : 2 * TILE, :] = low

        def sample(i, comp=comp):
            part = pl.ds(pl.multiple_of(i * turn, turn), turn)
            cells = lax.broadcasted_iota(jnp.int32, (TILE, turn), 0)
            near = jnp.dot(parts[...], on_rows[:, part], preferred_element_type=f32)
            near = near[0:TILE] + near[TILE : 2 * TILE]
            kick = jnp.sum(
                jnp.where(cells == col_ref[:, part], near, f32(0)), axis=0, keepdims=True
            )
            out_ref[comp : comp + 1, part] = momenta_ref[comp : comp + 1, part] + kick

        each(0, count // turn, sample)

    for exchange in (EX_A, EX_B, EX_Z):
        all_of(exchange).wait_send()
    for comp in range(2):
        for exchange in (EX_C, EX_P, EX_D):
            all_of(exchange, comp).wait_send()


def shards(cell_row, cell_col, weights, momenta):
    count = cell_row.shape[1]
    dma = pltpu.SemaphoreType.DMA
    base = base_tables()
    kicked = pl.pallas_call(
        collide_kernel,
        out_shape=jax.ShapeDtypeStruct((2, count), f32),
        in_specs=[pl.BlockSpec(memory_space=pltpu.HBM)] * 5,
        out_specs=pl.BlockSpec(memory_space=pltpu.VMEM),
        scratch_shapes=[
            pltpu.VMEM((1, count), jnp.int32),
            pltpu.VMEM((1, count), jnp.int32),
            pltpu.VMEM((1, count), f32),
            pltpu.VMEM((2, count), f32),
            pltpu.VMEM(base.shape, f32),
            pltpu.VMEM((TILE, count), bf16),
            pltpu.VMEM((2 * TILE, TILE), f32),
            pltpu.VMEM((PLANE, SHARE, TILE), f32),
            pltpu.VMEM((2, BLOCKS, TILE, TILE), bf16),
            pltpu.VMEM((TILE, TILE), bf16),
            pltpu.VMEM((TILE, TILE), bf16),
            pltpu.VMEM((PLANE, SHARE, TILE), f32),
            pltpu.VMEM((PLANE, SHARE, HALF), f32),
            pltpu.VMEM((PLANE, SHARE, HALF), f32),
            pltpu.VMEM((RING, SHARE, TILE), f32),
            pltpu.VMEM((RING, SHARE, TILE), f32),
            pltpu.VMEM((2, BLOCKS, SHARE, TILE), f32),
            pltpu.VMEM((2, RING, SHARE, TILE), f32),
            pltpu.VMEM((2, RING, SHARE, TILE), f32),
            pltpu.VMEM((2, PLANE, SHARE, HALF), f32),
            pltpu.VMEM((2, PLANE, SHARE, HALF), f32),
            pltpu.VMEM((2, BLOCKS, SHARE, TILE), f32),
            pltpu.VMEM((2, PLANE, SHARE, TILE), f32),
            pltpu.VMEM((2 * TILE, TILE), bf16),
            dma((5,)), dma((EXCHANGES,)), dma((EXCHANGES,)),
        ],
        compiler_params=pltpu.CompilerParams(
            vmem_limit_bytes=48 * 1024 * 1024, collective_id=0, has_side_effects=True
        ),
        name="collide",
    )(
        *[
            pltpu.with_memory_space_constraint(array, pltpu.HBM)
            for array in (cell_row, cell_col, weights, momenta[0], jnp.asarray(base))
        ]
    )
    return kicked[None]


def solution(mesh):
    placed = (
        P("beam", ("tx", "ty", "dom")),
        P("beam", ("tx", "ty", "dom")),
        P("beam", ("tx", "ty", "dom")),
        P("beam", None, ("tx", "ty", "dom")),
    )
    return jax.shard_map(
        shards,
        mesh=mesh,
        in_specs=placed,
        out_specs=P("beam", None, ("tx", "ty", "dom")),
        check_vma=False,
    )
```

```python
import jax
import jax.numpy as jnp
import numpy as np
from jax import lax
from jax.experimental import pallas as pl
from jax.experimental.pallas import tpu as pltpu
from jax.sharding import PartitionSpec as P

GRID = 2048
TILE = 256
BLOCKS = 8
SHARE = 16
PLANE = 16
RING = 8
HALF = 128
DEPOSIT_STEP = 8192
SAMPLE_STEP = 8192
kick_gain = 2.0
f32 = jnp.float32
bf16 = jnp.bfloat16

COARSE_SIN, COARSE_COS, FINE_SIN, FINE_COS, CENTRE_SIN, CENTRE_COS, EIGEN, WAVE = (
    0, 8, 16, 32, 48, 56, 64, 65,
)
BASE_ROWS = 72

EX_A, EX_B, EX_Z, EX_C, EX_P, EX_D, EXCHANGES = 0, 1, 2, 3, 5, 7, 9


def base_tables():
    points = GRID + 1
    wave = np.arange(1, GRID + 1, dtype=np.int64)

    def angles(doubled):
        doubled = np.asarray(doubled, dtype=np.int64)
        return np.pi * ((doubled[:, None] * wave[None, :]) % (4 * points)) / (2 * points)

    coarse = angles(32 * np.arange(8))
    fine = angles(2 * np.arange(16) + 1)
    centre = angles(2 * TILE * np.arange(BLOCKS) + TILE + 1)
    rows = np.zeros((BASE_ROWS, GRID))
    rows[0:64] = np.concatenate(
        [np.sin(coarse), np.cos(coarse), np.sin(fine), np.cos(fine), np.sin(centre), np.cos(centre)]
    )
    rows[EIGEN] = 4.0 * np.sin(np.pi * wave / (2 * points)) ** 2
    rows[WAVE] = np.pi * wave / points
    blocks = rows.reshape(BASE_ROWS, BLOCKS, TILE).transpose(1, 0, 2)
    return np.ascontiguousarray(blocks).astype(np.float32)


def split(x):
    high = x.astype(bf16)
    low = (x - high.astype(f32)).astype(bf16)
    return high, low


def collide_kernel(
    row_hbm, col_hbm, weight_hbm, momenta_hbm, base_hbm, out_ref,
    row_ref, col_ref, weight_ref, momenta_ref, base_ref,
    on_rows, total, tile_out, tables, even, odd, charge_in, modes_out, modes_in, turned_out,
    spectrum_in, scaled, column_out, column_in, back_out, back_in, field_out, field_in, parts,
    load, sent, came,
):
    beam, tx = lax.axis_index("beam"), lax.axis_index("tx")
    ty, dom = lax.axis_index("ty"), lax.axis_index("dom")
    here = tx * 2 + dom
    count = row_ref.shape[1]

    loads = [
        pltpu.make_async_copy(src, dst, load.at[i])
        for i, (src, dst) in enumerate(
            [
                (row_hbm, row_ref), (col_hbm, col_ref), (weight_hbm, weight_ref),
                (base_hbm, base_ref), (momenta_hbm, momenta_ref),
            ]
        )
    ]
    for item in loads:
        item.start()

    def each(first, last, act):
        def body(i, carry):
            act(i)
            return carry

        lax.fori_loop(first, last, body, 0)

    def plane_id(peer):
        return {"tx": lax.div(peer, 2), "dom": lax.rem(peer, 2)}

    def other_id(peer):
        return {"beam": 1 - beam, "ty": peer}

    def ring_id(peer):
        return {"ty": peer}

    def hops(distance, size):
        return min(distance, size - distance)

    steps = [(dy, dx) for dy in range(4) for dx in range(4)]
    steps.sort(key=lambda step: -hops(step[0], 4) - hops(step[1], 4))
    plane_others = [
        lax.rem(lax.div(here, 4) + dy, 4) * 4 + lax.rem(lax.rem(here, 4) + dx, 4)
        for dy, dx in steps[:-1]
    ]
    ring_all = [
        lax.rem(ty + step, RING)
        for step in sorted(range(RING), key=lambda step: -hops(step, RING))
    ]
    ring_others = ring_all[:-1]

    def copy(src, dst, exchange, device):
        return pltpu.make_async_remote_copy(
            src_ref=src, dst_ref=dst, send_sem=sent.at[exchange], recv_sem=came.at[exchange],
            device_id=device, device_id_type=pl.DeviceIdType.MESH,
        )

    mine_in = dom * BLOCKS + tx

    def to_a(peer):
        return copy(tile_out.at[peer], charge_in.at[mine_in], EX_A, plane_id(peer))

    def to_b(peer):
        return copy(modes_out.at[peer], modes_in.at[here], EX_B, plane_id(peer))

    def to_z(peer):
        return copy(turned_out.at[peer], spectrum_in.at[ty], EX_Z, other_id(peer))

    def to_c(comp, peer):
        return copy(
            column_out.at[comp, peer], column_in.at[comp, ty], EX_C + comp, ring_id(peer)
        )

    def to_p(comp, peer):
        return copy(back_out.at[comp, peer], back_in.at[comp, here], EX_P + comp, plane_id(peer))

    def to_d(comp, peer):
        return copy(
            field_out.at[comp, lax.div(peer, 2)], field_in.at[comp, here],
            EX_D + comp, plane_id(peer),
        )

    others, rest = pl.ds(0, PLANE - 1), pl.ds(0, RING - 1)

    def all_of(exchange, comp=0):
        slots = {
            EX_A: charge_in.at[others],
            EX_B: modes_in.at[others],
            EX_Z: spectrum_in,
            EX_C: column_in.at[comp, rest],
            EX_P: back_in.at[comp, others],
            EX_D: field_in.at[comp, others],
        }[exchange]
        device = ring_id(ring_others[0]) if exchange in (EX_Z, EX_C) else plane_id(plane_others[0])
        return copy(slots, slots, exchange + comp, device)

    barrier = pltpu.get_barrier_semaphore()

    def greet(device):
        pl.semaphore_signal(
            barrier, inc=1, device_id=device, device_id_type=pl.DeviceIdType.MESH
        )

    for peer in ring_all:
        greet(other_id(peer))
    for peer in plane_others:
        greet(plane_id(peer))
    for peer in ring_others:
        greet(ring_id(peer))

    total[...] = jnp.zeros_like(total)
    for item in loads[0:3]:
        item.wait()
    step = min(DEPOSIT_STEP, count)

    def deposit(i):
        part = pl.ds(pl.multiple_of(i * step, step), step)
        cells = lax.broadcasted_iota(jnp.int32, (TILE, step), 0).astype(f32).astype(bf16)
        high, low = split(weight_ref[:, part])
        on_row = jnp.where(
            cells == row_ref[:, part].astype(f32).astype(bf16), bf16(1), bf16(0)
        )
        on_rows[:, part] = on_row
        hit = cells == col_ref[:, part].astype(f32).astype(bf16)
        on_col = jnp.concatenate(
            [jnp.where(hit, high, bf16(0)), jnp.where(hit, low, bf16(0))], axis=0
        )
        total[...] += lax.dot_general(
            on_col, on_row, (((1,), (1,)), ((), ())), preferred_element_type=f32
        )

    each(0, count // step, deposit)
    tile = total[0:TILE, :] + total[TILE : 2 * TILE, :]
    tile = 0.75 * tile + 0.25 * pltpu.roll(tile, 1, 1)
    tile = 0.625 * tile + 0.375 * pltpu.roll(tile, 1, 0)
    tile_out[...] = tile.reshape(PLANE, SHARE, TILE)

    pl.semaphore_wait(barrier, PLANE - 1 + RING + RING - 1)
    for peer in plane_others:
        to_a(peer).start()
    charge_in[mine_in] = tile_out[here]

    loads[3].wait()

    def fill(j):
        fine_sin = base_ref[j, FINE_SIN : FINE_SIN + 16, :]
        fine_cos = base_ref[j, FINE_COS : FINE_COS + 16, :]
        for a in range(8):
            coarse_sin = base_ref[j, COARSE_SIN + a : COARSE_SIN + a + 1, :]
            coarse_cos = base_ref[j, COARSE_COS + a : COARSE_COS + a + 1, :]
            pair = (
                coarse_sin * fine_cos + coarse_cos * fine_sin,
                coarse_cos * fine_cos - coarse_sin * fine_sin,
            )
            for kind in range(2):
                high, low = split(pair[kind])
                tables[kind, j, 16 * a : 16 * a + 16, :] = high
                tables[kind, j, HALF + 16 * a : HALF + 16 * a + 16, :] = low

    each(0, BLOCKS, fill)
    even[HALF:TILE, HALF:TILE] = jnp.zeros((HALF, HALF), bf16)
    odd[HALF:TILE, HALF:TILE] = jnp.zeros((HALF, HALF), bf16)

    def load_lines(left, right):
        backward = (HALF - 1) - lax.broadcasted_iota(jnp.int32, (HALF, HALF), 1)
        left = jnp.take_along_axis(left, backward, axis=1)
        for ref, folded in ((even, right + left), (odd, right - left)):
            high, low = split(folded)
            ref[0:HALF, 0:HALF] = high
            ref[0:HALF, HALF:TILE] = high
            ref[HALF:TILE, 0:HALF] = low

    def load_chunks(x):
        x = x.reshape(BLOCKS * SHARE, TILE)
        load_lines(x[:, 0:HALF], x[:, HALF:TILE])

    def transform(j, cosine):
        by_sin = jnp.dot(odd[...], tables[0, j], preferred_element_type=f32)
        by_cos = jnp.dot(even[...], tables[1, j], preferred_element_type=f32)
        by_sin = by_sin[0:HALF] + by_sin[HALF:TILE]
        by_cos = by_cos[0:HALF] + by_cos[HALF:TILE]
        result = None
        for chunk in range(BLOCKS):
            rows = slice(SHARE * chunk, SHARE * chunk + SHARE)
            centre_sin = base_ref[j, CENTRE_SIN + chunk : CENTRE_SIN + chunk + 1, :]
            centre_cos = base_ref[j, CENTRE_COS + chunk : CENTRE_COS + chunk + 1, :]
            if cosine:
                term = centre_cos * by_cos[rows] - centre_sin * by_sin[rows]
            else:
                term = centre_sin * by_cos[rows] + centre_cos * by_sin[rows]
            result = term if result is None else result + term
        return result

    all_of(EX_A).wait_recv()
    load_chunks(charge_in[0:BLOCKS] + charge_in[BLOCKS : 2 * BLOCKS])
    for j in range(BLOCKS):
        modes = transform(j, False)
        modes_out[2 * j] = modes[:, 0:HALF]
        modes_out[2 * j + 1] = modes[:, HALF:TILE]
    for peer in plane_others:
        to_b(peer).start()
    modes_in[here] = modes_out[here]

    first_mode = here * HALF + ty * SHARE
    lane = lax.broadcasted_iota(jnp.int32, (SHARE, TILE), 1)
    sublane = lax.broadcasted_iota(jnp.int32, (SHARE, TILE), 0)
    mine = lane == sublane + lax.rem(first_mode, TILE)
    my_block = lax.div(first_mode, TILE)

    def of_mine(row):
        values = base_ref[my_block, row : row + 1, :]
        return jnp.sum(jnp.where(mine, values, f32(0)), axis=1, keepdims=True)

    my_eigen, my_wave = of_mine(EIGEN), of_mine(WAVE)

    all_of(EX_B).wait_recv()
    turned_out[...] = modes_in[...].reshape(TILE, HALF).T.reshape(RING, SHARE, TILE)
    for peer in ring_all:
        to_z(peer).start()

    all_of(EX_Z).wait_recv()
    load_chunks(spectrum_in[...])
    scale = f32((2.0 / (GRID + 1)) ** 2)
    for j in range(BLOCKS):
        potential = transform(j, False) * scale / (my_eigen + base_ref[j, EIGEN : EIGEN + 1, :])
        scaled[0, j] = -my_wave * potential
        scaled[1, j] = -base_ref[j, WAVE : WAVE + 1, :] * potential

    def column_back(comp):
        load_chunks(scaled[comp])
        for j in range(BLOCKS):
            column_out[comp, j] = transform(j, comp == 1)

    def send_c(comp):
        for peer in ring_others:
            to_c(comp, peer).start()
        column_in[comp, ty] = column_out[comp, ty]

    def send_p(comp):
        all_of(EX_C, comp).wait_recv()
        back_out[comp] = column_in[comp].reshape(HALF, TILE).T.reshape(PLANE, SHARE, HALF)
        for peer in plane_others:
            to_p(comp, peer).start()
        back_in[comp, here] = back_out[comp, here]

    def send_d(comp):
        all_of(EX_P, comp).wait_recv()
        load_lines(
            jnp.concatenate([back_in[comp, 2 * j] for j in range(BLOCKS)], axis=0),
            jnp.concatenate([back_in[comp, 2 * j + 1] for j in range(BLOCKS)], axis=0),
        )
        for j in range(BLOCKS):
            field_out[comp, j] = transform(j, comp == 0)
        for peer in plane_others:
            to_d(comp, peer).start()
        field_in[comp, here] = field_out[comp, tx]

    column_back(0)
    send_c(0)
    column_back(1)
    send_p(0)
    send_c(1)
    send_d(0)
    send_p(1)
    send_d(1)

    loads[4].wait()
    turn = min(SAMPLE_STEP, count)
    for comp in range(2):
        all_of(EX_D, comp).wait_recv()
        field = field_in[comp].reshape(TILE, TILE)
        field = 0.75 * field + 0.25 * pltpu.roll(field, TILE - 1, 1)
        field = kick_gain * (0.625 * field + 0.375 * pltpu.roll(field, TILE - 1, 0))
        high, low = split(field)
        parts[0:TILE, :] = high
        parts[TILE : 2 * TILE, :] = low

        def sample(i, comp=comp):
            part = pl.ds(pl.multiple_of(i * turn, turn), turn)
            cells = lax.broadcasted_iota(jnp.int32, (TILE, turn), 0)
            near = jnp.dot(parts[...], on_rows[:, part], preferred_element_type=f32)
            near = near[0:TILE] + near[TILE : 2 * TILE]
            kick = jnp.sum(
                jnp.where(cells == col_ref[:, part], near, f32(0)), axis=0, keepdims=True
            )
            out_ref[comp : comp + 1, part] = momenta_ref[comp : comp + 1, part] + kick

        each(0, count // turn, sample)

    for exchange in (EX_A, EX_B, EX_Z):
        all_of(exchange).wait_send()
    for comp in range(2):
        for exchange in (EX_C, EX_P, EX_D):
            all_of(exchange, comp).wait_send()


def shards(cell_row, cell_col, weights, momenta):
    count = cell_row.shape[1]
    dma = pltpu.SemaphoreType.DMA
    base = base_tables()
    kicked = pl.pallas_call(
        collide_kernel,
        out_shape=jax.ShapeDtypeStruct((2, count), f32),
        in_specs=[pl.BlockSpec(memory_space=pltpu.HBM)] * 5,
        out_specs=pl.BlockSpec(memory_space=pltpu.VMEM),
        scratch_shapes=[
            pltpu.VMEM((1, count), jnp.int32),
            pltpu.VMEM((1, count), jnp.int32),
            pltpu.VMEM((1, count), f32),
            pltpu.VMEM((2, count), f32),
            pltpu.VMEM(base.shape, f32),
            pltpu.VMEM((TILE, count), bf16),
            pltpu.VMEM((2 * TILE, TILE), f32),
            pltpu.VMEM((PLANE, SHARE, TILE), f32),
            pltpu.VMEM((2, BLOCKS, TILE, TILE), bf16),
            pltpu.VMEM((TILE, TILE), bf16),
            pltpu.VMEM((TILE, TILE), bf16),
            pltpu.VMEM((PLANE, SHARE, TILE), f32),
            pltpu.VMEM((PLANE, SHARE, HALF), f32),
            pltpu.VMEM((PLANE, SHARE, HALF), f32),
            pltpu.VMEM((RING, SHARE, TILE), f32),
            pltpu.VMEM((RING, SHARE, TILE), f32),
            pltpu.VMEM((2, BLOCKS, SHARE, TILE), f32),
            pltpu.VMEM((2, RING, SHARE, TILE), f32),
            pltpu.VMEM((2, RING, SHARE, TILE), f32),
            pltpu.VMEM((2, PLANE, SHARE, HALF), f32),
            pltpu.VMEM((2, PLANE, SHARE, HALF), f32),
            pltpu.VMEM((2, BLOCKS, SHARE, TILE), f32),
            pltpu.VMEM((2, PLANE, SHARE, TILE), f32),
            pltpu.VMEM((2 * TILE, TILE), bf16),
            dma((5,)), dma((EXCHANGES,)), dma((EXCHANGES,)),
        ],
        compiler_params=pltpu.CompilerParams(
            vmem_limit_bytes=48 * 1024 * 1024, collective_id=0, has_side_effects=True
        ),
        name="collide",
    )(
        *[
            pltpu.with_memory_space_constraint(array, pltpu.HBM)
            for array in (cell_row, cell_col, weights, momenta[0], jnp.asarray(base))
        ]
    )
    return kicked[None]


def solution(mesh):
    placed = (
        P("beam", ("tx", "ty", "dom")),
        P("beam", ("tx", "ty", "dom")),
        P("beam", ("tx", "ty", "dom")),
        P("beam", None, ("tx", "ty", "dom")),
    )
    return jax.shard_map(
        shards,
        mesh=mesh,
        in_specs=placed,
        out_specs=P("beam", None, ("tx", "ty", "dom")),
        check_vma=False,
    )
```

```python
import jax
import jax.numpy as jnp
import numpy as np
from jax import lax
from jax.experimental import pallas as pl
from jax.experimental.pallas import tpu as pltpu
from jax.sharding import PartitionSpec as P

GRID = 2048
TILE = 256
BLOCKS = 8
SHARE = 16
PLANE = 16
RING = 8
HALF = 128
DEPOSIT_STEP = 8192
SAMPLE_STEP = 8192
kick_gain = 2.0
f32 = jnp.float32
bf16 = jnp.bfloat16

COARSE_SIN, COARSE_COS, FINE_SIN, FINE_COS, CENTRE_SIN, CENTRE_COS, EIGEN, WAVE = (
    0, 8, 16, 32, 48, 56, 64, 65,
)
BASE_ROWS = 72

EX_A, EX_B, EX_Z, EX_C, EX_P, EX_D, EXCHANGES = 0, 1, 2, 3, 5, 7, 9


def base_tables():
    points = GRID + 1
    wave = np.arange(1, GRID + 1, dtype=np.int64)

    def angles(doubled):
        doubled = np.asarray(doubled, dtype=np.int64)
        return np.pi * ((doubled[:, None] * wave[None, :]) % (4 * points)) / (2 * points)

    coarse = angles(32 * np.arange(8))
    fine = angles(2 * np.arange(16) + 1)
    centre = angles(2 * TILE * np.arange(BLOCKS) + TILE + 1)
    rows = np.zeros((BASE_ROWS, GRID))
    rows[0:64] = np.concatenate(
        [np.sin(coarse), np.cos(coarse), np.sin(fine), np.cos(fine), np.sin(centre), np.cos(centre)]
    )
    rows[EIGEN] = 4.0 * np.sin(np.pi * wave / (2 * points)) ** 2
    rows[WAVE] = np.pi * wave / points
    blocks = rows.reshape(BASE_ROWS, BLOCKS, TILE).transpose(1, 0, 2)
    return np.ascontiguousarray(blocks).astype(np.float32)


def split(x):
    high = x.astype(bf16)
    low = (x - high.astype(f32)).astype(bf16)
    return high, low


def collide_kernel(
    row_hbm, col_hbm, weight_hbm, momenta_hbm, base_hbm, out_ref,
    row_ref, col_ref, weight_ref, momenta_ref, base_ref,
    on_rows, total, tile_out, tables, even, odd, charge_in, modes_out, modes_in, turned_out,
    spectrum_in, scaled, column_out, column_in, back_out, back_in, field_out, field_in, parts,
    load, sent, came,
):
    beam, tx = lax.axis_index("beam"), lax.axis_index("tx")
    ty, dom = lax.axis_index("ty"), lax.axis_index("dom")
    here = tx * 2 + dom
    count = row_ref.shape[1]

    loads = [
        pltpu.make_async_copy(src, dst, load.at[i])
        for i, (src, dst) in enumerate(
            [
                (row_hbm, row_ref), (col_hbm, col_ref), (weight_hbm, weight_ref),
                (base_hbm, base_ref), (momenta_hbm, momenta_ref),
            ]
        )
    ]
    for item in loads[0:3]:
        item.start()

    def each(first, last, act):
        def body(i, carry):
            act(i)
            return carry

        lax.fori_loop(first, last, body, 0)

    def plane_id(peer):
        return {"tx": lax.div(peer, 2), "dom": lax.rem(peer, 2)}

    def other_id(peer):
        return {"beam": 1 - beam, "tx": lax.div(peer, 2), "dom": lax.rem(peer, 2)}

    def ring_id(peer):
        return {"ty": peer}

    def hops(distance, size):
        return min(distance, size - distance)

    steps = [(dy, dx) for dy in range(4) for dx in range(4)]
    steps.sort(key=lambda step: -hops(step[0], 4) - hops(step[1], 4))
    plane_all = [
        lax.rem(lax.div(here, 4) + dy, 4) * 4 + lax.rem(lax.rem(here, 4) + dx, 4)
        for dy, dx in steps
    ]
    plane_others = plane_all[:-1]
    ring_others = [
        lax.rem(ty + step, RING)
        for step in sorted(range(1, RING), key=lambda step: -hops(step, RING))
    ]

    def copy(src, dst, exchange, device):
        return pltpu.make_async_remote_copy(
            src_ref=src, dst_ref=dst, send_sem=sent.at[exchange], recv_sem=came.at[exchange],
            device_id=device, device_id_type=pl.DeviceIdType.MESH,
        )

    mine_in = dom * BLOCKS + tx

    def to_a(peer):
        return copy(tile_out.at[peer], charge_in.at[mine_in], EX_A, plane_id(peer))

    def to_b(peer):
        return copy(modes_out.at[peer], modes_in.at[here], EX_B, other_id(peer))

    def to_z(peer):
        return copy(turned_out.at[peer], spectrum_in.at[ty], EX_Z, ring_id(peer))

    def to_c(comp, peer):
        return copy(
            column_out.at[comp, peer], column_in.at[comp, ty], EX_C + comp, ring_id(peer)
        )

    def to_p(comp, peer):
        return copy(back_out.at[comp, peer], back_in.at[comp, here], EX_P + comp, plane_id(peer))

    def to_d(comp, peer):
        return copy(
            field_out.at[comp, lax.div(peer, 2)], field_in.at[comp, here],
            EX_D + comp, plane_id(peer),
        )

    others, rest = pl.ds(0, PLANE - 1), pl.ds(0, RING - 1)

    def all_of(exchange, comp=0):
        slots = {
            EX_A: charge_in.at[others],
            EX_B: modes_in,
            EX_Z: spectrum_in.at[rest],
            EX_C: column_in.at[comp, rest],
            EX_P: back_in.at[comp, others],
            EX_D: field_in.at[comp, others],
        }[exchange]
        device = ring_id(ring_others[0]) if exchange in (EX_Z, EX_C) else plane_id(plane_others[0])
        return copy(slots, slots, exchange + comp, device)

    barrier = pltpu.get_barrier_semaphore()

    def greet(device):
        pl.semaphore_signal(
            barrier, inc=1, device_id=device, device_id_type=pl.DeviceIdType.MESH
        )

    for peer in plane_all:
        greet(other_id(peer))
    for peer in plane_others:
        greet(plane_id(peer))
    for peer in ring_others:
        greet(ring_id(peer))

    total[...] = jnp.zeros_like(total)
    for item in loads[0:3]:
        item.wait()
    for item in loads[3:5]:
        item.start()
    step = min(DEPOSIT_STEP, count)

    def deposit(i):
        part = pl.ds(pl.multiple_of(i * step, step), step)
        cells = lax.broadcasted_iota(jnp.int32, (TILE, step), 0).astype(f32).astype(bf16)
        high, low = split(weight_ref[:, part])
        on_row = jnp.where(
            cells == row_ref[:, part].astype(f32).astype(bf16), bf16(1), bf16(0)
        )
        on_rows[:, part] = on_row
        hit = cells == col_ref[:, part].astype(f32).astype(bf16)
        on_col = jnp.concatenate(
            [jnp.where(hit, high, bf16(0)), jnp.where(hit, low, bf16(0))], axis=0
        )
        total[...] += lax.dot_general(
            on_col, on_row, (((1,), (1,)), ((), ())), preferred_element_type=f32
        )

    each(0, count // step, deposit)
    tile = total[0:TILE, :] + total[TILE : 2 * TILE, :]
    tile = 0.75 * tile + 0.25 * pltpu.roll(tile, 1, 1)
    tile = 0.625 * tile + 0.375 * pltpu.roll(tile, 1, 0)
    tile_out[...] = tile.reshape(PLANE, SHARE, TILE)

    pl.semaphore_wait(barrier, PLANE + PLANE - 1 + RING - 1)
    for peer in plane_others:
        to_a(peer).start()
    charge_in[mine_in] = tile_out[here]

    loads[3].wait()

    def fill(j):
        fine_sin = base_ref[j, FINE_SIN : FINE_SIN + 16, :]
        fine_cos = base_ref[j, FINE_COS : FINE_COS + 16, :]
        for a in range(8):
            coarse_sin = base_ref[j, COARSE_SIN + a : COARSE_SIN + a + 1, :]
            coarse_cos = base_ref[j, COARSE_COS + a : COARSE_COS + a + 1, :]
            pair = (
                coarse_sin * fine_cos + coarse_cos * fine_sin,
                coarse_cos * fine_cos - coarse_sin * fine_sin,
            )
            for kind in range(2):
                high, low = split(pair[kind])
                tables[kind, j, 16 * a : 16 * a + 16, :] = high
                tables[kind, j, HALF + 16 * a : HALF + 16 * a + 16, :] = low

    each(0, BLOCKS, fill)
    even[HALF:TILE, HALF:TILE] = jnp.zeros((HALF, HALF), bf16)
    odd[HALF:TILE, HALF:TILE] = jnp.zeros((HALF, HALF), bf16)

    def load_lines(left, right):
        backward = (HALF - 1) - lax.broadcasted_iota(jnp.int32, (HALF, HALF), 1)
        left = jnp.take_along_axis(left, backward, axis=1)
        for ref, folded in ((even, right + left), (odd, right - left)):
            high, low = split(folded)
            ref[0:HALF, 0:HALF] = high
            ref[0:HALF, HALF:TILE] = high
            ref[HALF:TILE, 0:HALF] = low

    def load_chunks(x):
        x = x.reshape(BLOCKS * SHARE, TILE)
        load_lines(x[:, 0:HALF], x[:, HALF:TILE])

    def transform(j, cosine):
        by_sin = jnp.dot(odd[...], tables[0, j], preferred_element_type=f32)
        by_cos = jnp.dot(even[...], tables[1, j], preferred_element_type=f32)
        by_sin = by_sin[0:HALF] + by_sin[HALF:TILE]
        by_cos = by_cos[0:HALF] + by_cos[HALF:TILE]
        result = None
        for chunk in range(BLOCKS):
            rows = slice(SHARE * chunk, SHARE * chunk + SHARE)
            centre_sin = base_ref[j, CENTRE_SIN + chunk : CENTRE_SIN + chunk + 1, :]
            centre_cos = base_ref[j, CENTRE_COS + chunk : CENTRE_COS + chunk + 1, :]
            if cosine:
                term = centre_cos * by_cos[rows] - centre_sin * by_sin[rows]
            else:
                term = centre_sin * by_cos[rows] + centre_cos * by_sin[rows]
            result = term if result is None else result + term
        return result

    all_of(EX_A).wait_recv()
    load_chunks(charge_in[0:BLOCKS] + charge_in[BLOCKS : 2 * BLOCKS])
    for j in range(BLOCKS):
        modes = transform(j, False)
        modes_out[2 * j] = modes[:, 0:HALF]
        modes_out[2 * j + 1] = modes[:, HALF:TILE]
    for peer in plane_all:
        to_b(peer).start()

    first_mode = here * HALF + ty * SHARE
    lane = lax.broadcasted_iota(jnp.int32, (SHARE, TILE), 1)
    sublane = lax.broadcasted_iota(jnp.int32, (SHARE, TILE), 0)
    mine = lane == sublane + lax.rem(first_mode, TILE)
    my_block = lax.div(first_mode, TILE)

    def of_mine(row):
        values = base_ref[my_block, row : row + 1, :]
        return jnp.sum(jnp.where(mine, values, f32(0)), axis=1, keepdims=True)

    my_eigen, my_wave = of_mine(EIGEN), of_mine(WAVE)

    all_of(EX_B).wait_recv()
    turned_out[...] = modes_in[...].reshape(TILE, HALF).T.reshape(RING, SHARE, TILE)
    for peer in ring_others:
        to_z(peer).start()
    spectrum_in[ty] = turned_out[ty]

    all_of(EX_Z).wait_recv()
    load_chunks(spectrum_in[...])
    scale = f32((2.0 / (GRID + 1)) ** 2)
    for j in range(BLOCKS):
        potential = transform(j, False) * scale / (my_eigen + base_ref[j, EIGEN : EIGEN + 1, :])
        scaled[0, j] = -my_wave * potential
        scaled[1, j] = -base_ref[j, WAVE : WAVE + 1, :] * potential

    for comp in range(2):
        load_chunks(scaled[comp])
        for j in range(BLOCKS):
            column_out[comp, j] = transform(j, comp == 1)
        for peer in ring_others:
            to_c(comp, peer).start()
        column_in[comp, ty] = column_out[comp, ty]

    for comp in range(2):
        all_of(EX_C, comp).wait_recv()
        back_out[comp] = column_in[comp].reshape(HALF, TILE).T.reshape(PLANE, SHARE, HALF)
        for peer in plane_others:
            to_p(comp, peer).start()
        back_in[comp, here] = back_out[comp, here]

    for comp in range(2):
        all_of(EX_P, comp).wait_recv()
        load_lines(
            jnp.concatenate([back_in[comp, 2 * j] for j in range(BLOCKS)], axis=0),
            jnp.concatenate([back_in[comp, 2 * j + 1] for j in range(BLOCKS)], axis=0),
        )
        for j in range(BLOCKS):
            field_out[comp, j] = transform(j, comp == 0)
        for peer in plane_others:
            to_d(comp, peer).start()
        field_in[comp, here] = field_out[comp, tx]

    loads[4].wait()
    turn = min(SAMPLE_STEP, count)
    for comp in range(2):
        all_of(EX_D, comp).wait_recv()
        field = field_in[comp].reshape(TILE, TILE)
        field = 0.75 * field + 0.25 * pltpu.roll(field, TILE - 1, 1)
        field = kick_gain * (0.625 * field + 0.375 * pltpu.roll(field, TILE - 1, 0))
        high, low = split(field)
        parts[0:TILE, :] = high
        parts[TILE : 2 * TILE, :] = low

        def sample(i, comp=comp):
            part = pl.ds(pl.multiple_of(i * turn, turn), turn)
            cells = lax.broadcasted_iota(jnp.int32, (TILE, turn), 0)
            near = jnp.dot(parts[...], on_rows[:, part], preferred_element_type=f32)
            near = near[0:TILE] + near[TILE : 2 * TILE]
            kick = jnp.sum(
                jnp.where(cells == col_ref[:, part], near, f32(0)), axis=0, keepdims=True
            )
            out_ref[comp : comp + 1, part] = momenta_ref[comp : comp + 1, part] + kick

        each(0, count // turn, sample)

    for exchange in (EX_A, EX_B, EX_Z):
        all_of(exchange).wait_send()
    for comp in range(2):
        for exchange in (EX_C, EX_P, EX_D):
            all_of(exchange, comp).wait_send()


def shards(cell_row, cell_col, weights, momenta):
    count = cell_row.shape[1]
    dma = pltpu.SemaphoreType.DMA
    base = base_tables()
    kicked = pl.pallas_call(
        collide_kernel,
        out_shape=jax.ShapeDtypeStruct((2, count), f32),
        in_specs=[pl.BlockSpec(memory_space=pltpu.HBM)] * 5,
        out_specs=pl.BlockSpec(memory_space=pltpu.VMEM),
        scratch_shapes=[
            pltpu.VMEM((1, count), jnp.int32),
            pltpu.VMEM((1, count), jnp.int32),
            pltpu.VMEM((1, count), f32),
            pltpu.VMEM((2, count), f32),
            pltpu.VMEM(base.shape, f32),
            pltpu.VMEM((TILE, count), bf16),
            pltpu.VMEM((2 * TILE, TILE), f32),
            pltpu.VMEM((PLANE, SHARE, TILE), f32),
            pltpu.VMEM((2, BLOCKS, TILE, TILE), bf16),
            pltpu.VMEM((TILE, TILE), bf16),
            pltpu.VMEM((TILE, TILE), bf16),
            pltpu.VMEM((PLANE, SHARE, TILE), f32),
            pltpu.VMEM((PLANE, SHARE, HALF), f32),
            pltpu.VMEM((PLANE, SHARE, HALF), f32),
            pltpu.VMEM((RING, SHARE, TILE), f32),
            pltpu.VMEM((RING, SHARE, TILE), f32),
            pltpu.VMEM((2, BLOCKS, SHARE, TILE), f32),
            pltpu.VMEM((2, RING, SHARE, TILE), f32),
            pltpu.VMEM((2, RING, SHARE, TILE), f32),
            pltpu.VMEM((2, PLANE, SHARE, HALF), f32),
            pltpu.VMEM((2, PLANE, SHARE, HALF), f32),
            pltpu.VMEM((2, BLOCKS, SHARE, TILE), f32),
            pltpu.VMEM((2, PLANE, SHARE, TILE), f32),
            pltpu.VMEM((2 * TILE, TILE), bf16),
            dma((5,)), dma((EXCHANGES,)), dma((EXCHANGES,)),
        ],
        compiler_params=pltpu.CompilerParams(
            vmem_limit_bytes=48 * 1024 * 1024, collective_id=0, has_side_effects=True
        ),
        name="collide",
    )(
        *[
            pltpu.with_memory_space_constraint(array, pltpu.HBM)
            for array in (cell_row, cell_col, weights, momenta[0], jnp.asarray(base))
        ]
    )
    return kicked[None]


def solution(mesh):
    placed = (
        P("beam", ("tx", "ty", "dom")),
        P("beam", ("tx", "ty", "dom")),
        P("beam", ("tx", "ty", "dom")),
        P("beam", None, ("tx", "ty", "dom")),
    )
    return jax.shard_map(
        shards,
        mesh=mesh,
        in_specs=placed,
        out_specs=P("beam", None, ("tx", "ty", "dom")),
        check_vma=False,
    )
```

```python
import jax
import jax.numpy as jnp
import numpy as np
from jax import lax
from jax.experimental import pallas as pl
from jax.experimental.pallas import tpu as pltpu
from jax.sharding import PartitionSpec as P

GRID = 2048
TILE = 256
BLOCKS = 8
SHARE = 16
PLANE = 16
RING = 8
HALF = 128
DEPOSIT_STEP = 8192
SAMPLE_STEP = 8192
kick_gain = 2.0
f32 = jnp.float32
bf16 = jnp.bfloat16

COARSE_SIN, COARSE_COS, FINE_SIN, FINE_COS, CENTRE_SIN, CENTRE_COS, EIGEN, WAVE = (
    0, 8, 16, 32, 48, 56, 64, 65,
)
BASE_ROWS = 72

EX_A, EX_B, EX_Z, EX_C, EX_P, EX_D, EXCHANGES = 0, 1, 2, 3, 5, 7, 9


def base_tables():
    points = GRID + 1
    wave = np.arange(1, GRID + 1, dtype=np.int64)

    def angles(doubled):
        doubled = np.asarray(doubled, dtype=np.int64)
        return np.pi * ((doubled[:, None] * wave[None, :]) % (4 * points)) / (2 * points)

    coarse = angles(32 * np.arange(8))
    fine = angles(2 * np.arange(16) + 1)
    centre = angles(2 * TILE * np.arange(BLOCKS) + TILE + 1)
    rows = np.zeros((BASE_ROWS, GRID))
    rows[0:64] = np.concatenate(
        [np.sin(coarse), np.cos(coarse), np.sin(fine), np.cos(fine), np.sin(centre), np.cos(centre)]
    )
    rows[EIGEN] = 4.0 * np.sin(np.pi * wave / (2 * points)) ** 2
    rows[WAVE] = np.pi * wave / points
    blocks = rows.reshape(BASE_ROWS, BLOCKS, TILE).transpose(1, 0, 2)
    return np.ascontiguousarray(blocks).astype(np.float32)


def split(x):
    high = x.astype(bf16)
    low = (x - high.astype(f32)).astype(bf16)
    return high, low


def collide_kernel(
    row_hbm, col_hbm, weight_hbm, momenta_hbm, base_hbm, out_ref,
    row_ref, col_ref, weight_ref, momenta_ref, base_ref,
    on_rows, total, tile_out, tables, even, odd, charge_in, modes_out, modes_in, turned_out,
    spectrum_in, scaled, column_out, column_in, back_out, back_in, field_out, field_in, parts,
    load, sent, came,
):
    beam, tx = lax.axis_index("beam"), lax.axis_index("tx")
    ty, dom = lax.axis_index("ty"), lax.axis_index("dom")
    here = tx * 2 + dom
    count = row_ref.shape[1]

    loads = [
        pltpu.make_async_copy(src, dst, load.at[i])
        for i, (src, dst) in enumerate(
            [
                (row_hbm, row_ref), (col_hbm, col_ref), (weight_hbm, weight_ref),
                (base_hbm, base_ref), (momenta_hbm, momenta_ref),
            ]
        )
    ]
    for item in loads:
        item.start()

    def each(first, last, act):
        def body(i, carry):
            act(i)
            return carry

        lax.fori_loop(first, last, body, 0)

    def plane_id(peer):
        return {"tx": lax.div(peer, 2), "dom": lax.rem(peer, 2)}

    def other_id(peer):
        return {"beam": 1 - beam, "tx": lax.div(peer, 2), "dom": lax.rem(peer, 2)}

    def ring_id(peer):
        return {"ty": peer}

    def hops(distance, size):
        return min(distance, size - distance)

    steps = [(dy, dx) for dy in range(4) for dx in range(4)]
    steps.sort(key=lambda step: -hops(step[0], 4) - hops(step[1], 4))
    plane_all = [
        lax.rem(lax.div(here, 4) + dy, 4) * 4 + lax.rem(lax.rem(here, 4) + dx, 4)
        for dy, dx in steps
    ]
    plane_others = plane_all[:-1]
    ring_others = [
        lax.rem(ty + step, RING)
        for step in sorted(range(1, RING), key=lambda step: -hops(step, RING))
    ]

    def copy(src, dst, exchange, device):
        return pltpu.make_async_remote_copy(
            src_ref=src, dst_ref=dst, send_sem=sent.at[exchange], recv_sem=came.at[exchange],
            device_id=device, device_id_type=pl.DeviceIdType.MESH,
        )

    mine_in = dom * BLOCKS + tx

    def to_a(peer):
        return copy(tile_out.at[peer], charge_in.at[mine_in], EX_A, plane_id(peer))

    def to_b(peer):
        return copy(modes_out.at[peer], modes_in.at[here], EX_B, other_id(peer))

    def to_z(peer):
        return copy(turned_out.at[peer], spectrum_in.at[ty], EX_Z, ring_id(peer))

    def to_c(comp, peer):
        return copy(
            column_out.at[comp, peer], column_in.at[comp, ty], EX_C + comp, ring_id(peer)
        )

    def to_p(comp, peer):
        return copy(back_out.at[comp, peer], back_in.at[comp, here], EX_P + comp, plane_id(peer))

    def to_d(comp, peer):
        return copy(
            field_out.at[comp, lax.div(peer, 2)], field_in.at[comp, here],
            EX_D + comp, plane_id(peer),
        )

    others, rest = pl.ds(0, PLANE - 1), pl.ds(0, RING - 1)

    def all_of(exchange, comp=0):
        slots = {
            EX_A: charge_in.at[others],
            EX_B: modes_in,
            EX_Z: spectrum_in.at[rest],
            EX_C: column_in.at[comp, rest],
            EX_P: back_in.at[comp, others],
            EX_D: field_in.at[comp, others],
        }[exchange]
        device = ring_id(ring_others[0]) if exchange in (EX_Z, EX_C) else plane_id(plane_others[0])
        return copy(slots, slots, exchange + comp, device)

    barrier = pltpu.get_barrier_semaphore()

    def greet(device):
        pl.semaphore_signal(
            barrier, inc=1, device_id=device, device_id_type=pl.DeviceIdType.MESH
        )

    for peer in plane_all:
        greet(other_id(peer))
    for peer in plane_others:
        greet(plane_id(peer))
    for peer in ring_others:
        greet(ring_id(peer))

    total[...] = jnp.zeros_like(total)
    for item in loads[0:3]:
        item.wait()
    step = min(DEPOSIT_STEP, count)

    def deposit(i):
        part = pl.ds(pl.multiple_of(i * step, step), step)
        cells = lax.broadcasted_iota(jnp.int32, (TILE, step), 0).astype(f32).astype(bf16)
        high, low = split(weight_ref[:, part])
        on_row = jnp.where(
            cells == row_ref[:, part].astype(f32).astype(bf16), bf16(1), bf16(0)
        )
        on_rows[:, part] = on_row
        hit = cells == col_ref[:, part].astype(f32).astype(bf16)
        on_col = jnp.concatenate(
            [jnp.where(hit, high, bf16(0)), jnp.where(hit, low, bf16(0))], axis=0
        )
        total[...] += lax.dot_general(
            on_col, on_row, (((1,), (1,)), ((), ())), preferred_element_type=f32
        )

    each(0, count // step, deposit)
    tile = total[0:TILE, :] + total[TILE : 2 * TILE, :]
    tile = 0.75 * tile + 0.25 * pltpu.roll(tile, 1, 1)
    tile = 0.625 * tile + 0.375 * pltpu.roll(tile, 1, 0)
    tile_out[...] = tile.reshape(PLANE, SHARE, TILE)

    pl.semaphore_wait(barrier, PLANE + PLANE - 1 + RING - 1)
    for peer in plane_others:
        to_a(peer).start()
    charge_in[mine_in] = tile_out[here]

    loads[3].wait()

    def fill(j):
        fine_sin = base_ref[j, FINE_SIN : FINE_SIN + 16, :]
        fine_cos = base_ref[j, FINE_COS : FINE_COS + 16, :]
        for a in range(8):
            coarse_sin = base_ref[j, COARSE_SIN + a : COARSE_SIN + a + 1, :]
            coarse_cos = base_ref[j, COARSE_COS + a : COARSE_COS + a + 1, :]
            pair = (
                coarse_sin * fine_cos + coarse_cos * fine_sin,
                coarse_cos * fine_cos - coarse_sin * fine_sin,
            )
            for kind in range(2):
                high, low = split(pair[kind])
                tables[kind, j, 16 * a : 16 * a + 16, :] = high
                tables[kind, j, HALF + 16 * a : HALF + 16 * a + 16, :] = low

    each(0, BLOCKS, fill)
    even[HALF:TILE, HALF:TILE] = jnp.zeros((HALF, HALF), bf16)
    odd[HALF:TILE, HALF:TILE] = jnp.zeros((HALF, HALF), bf16)

    def load_lines(left, right):
        backward = (HALF - 1) - lax.broadcasted_iota(jnp.int32, (HALF, HALF), 1)
        left = jnp.take_along_axis(left, backward, axis=1)
        for ref, folded in ((even, right + left), (odd, right - left)):
            high, low = split(folded)
            ref[0:HALF, 0:HALF] = high
            ref[0:HALF, HALF:TILE] = high
            ref[HALF:TILE, 0:HALF] = low

    def load_chunks(x):
        x = x.reshape(BLOCKS * SHARE, TILE)
        load_lines(x[:, 0:HALF], x[:, HALF:TILE])

    def transform(j, cosine):
        by_sin = jnp.dot(odd[...], tables[0, j], preferred_element_type=f32)
        by_cos = jnp.dot(even[...], tables[1, j], preferred_element_type=f32)
        by_sin = by_sin[0:HALF] + by_sin[HALF:TILE]
        by_cos = by_cos[0:HALF] + by_cos[HALF:TILE]
        result = None
        for chunk in range(BLOCKS):
            rows = slice(SHARE * chunk, SHARE * chunk + SHARE)
            centre_sin = base_ref[j, CENTRE_SIN + chunk : CENTRE_SIN + chunk + 1, :]
            centre_cos = base_ref[j, CENTRE_COS + chunk : CENTRE_COS + chunk + 1, :]
            if cosine:
                term = centre_cos * by_cos[rows] - centre_sin * by_sin[rows]
            else:
                term = centre_sin * by_cos[rows] + centre_cos * by_sin[rows]
            result = term if result is None else result + term
        return result

    all_of(EX_A).wait_recv()
    load_chunks(charge_in[0:BLOCKS] + charge_in[BLOCKS : 2 * BLOCKS])
    for j in range(BLOCKS):
        modes = transform(j, False)
        modes_out[2 * j] = modes[:, 0:HALF]
        modes_out[2 * j + 1] = modes[:, HALF:TILE]
    for peer in plane_all:
        to_b(peer).start()

    first_mode = here * HALF + ty * SHARE
    lane = lax.broadcasted_iota(jnp.int32, (SHARE, TILE), 1)
    sublane = lax.broadcasted_iota(jnp.int32, (SHARE, TILE), 0)
    mine = lane == sublane + lax.rem(first_mode, TILE)
    my_block = lax.div(first_mode, TILE)

    def of_mine(row):
        values = base_ref[my_block, row : row + 1, :]
        return jnp.sum(jnp.where(mine, values, f32(0)), axis=1, keepdims=True)

    my_eigen, my_wave = of_mine(EIGEN), of_mine(WAVE)

    all_of(EX_B).wait_recv()
    turned_out[...] = modes_in[...].reshape(TILE, HALF).T.reshape(RING, SHARE, TILE)
    for peer in ring_others:
        to_z(peer).start()
    spectrum_in[ty] = turned_out[ty]

    all_of(EX_Z).wait_recv()
    load_chunks(spectrum_in[...])
    scale = f32((2.0 / (GRID + 1)) ** 2)
    for j in range(BLOCKS):
        potential = transform(j, False) * scale / (my_eigen + base_ref[j, EIGEN : EIGEN + 1, :])
        scaled[0, j] = -my_wave * potential
        scaled[1, j] = -base_ref[j, WAVE : WAVE + 1, :] * potential

    for comp in range(2):
        load_chunks(scaled[comp])
        for j in range(BLOCKS):
            column_out[comp, j] = transform(j, comp == 1)
        for peer in ring_others:
            to_c(comp, peer).start()
        column_in[comp, ty] = column_out[comp, ty]

    for comp in range(2):
        all_of(EX_C, comp).wait_recv()
        back_out[comp] = column_in[comp].reshape(HALF, TILE).T.reshape(PLANE, SHARE, HALF)
        for peer in plane_others:
            to_p(comp, peer).start()
        back_in[comp, here] = back_out[comp, here]

    for comp in range(2):
        all_of(EX_P, comp).wait_recv()
        load_lines(
            jnp.concatenate([back_in[comp, 2 * j] for j in range(BLOCKS)], axis=0),
            jnp.concatenate([back_in[comp, 2 * j + 1] for j in range(BLOCKS)], axis=0),
        )
        if comp == 0:
            for half in ((2, 1), (3, 0)):
                for dy in half:
                    for low in range(2):
                        j = lax.rem(lax.div(here, 4) + dy, 4) * 2 + low
                        field_out[comp, j] = transform(j, True)
                for step, peer in zip(steps[:-1], plane_others):
                    if step[0] in half:
                        to_d(comp, peer).start()
        else:
            for j in range(BLOCKS):
                field_out[comp, j] = transform(j, False)
            for peer in plane_others:
                to_d(comp, peer).start()
        field_in[comp, here] = field_out[comp, tx]

    loads[4].wait()
    turn = min(SAMPLE_STEP, count)
    for comp in range(2):
        all_of(EX_D, comp).wait_recv()
        field = field_in[comp].reshape(TILE, TILE)
        field = 0.75 * field + 0.25 * pltpu.roll(field, TILE - 1, 1)
        field = kick_gain * (0.625 * field + 0.375 * pltpu.roll(field, TILE - 1, 0))
        high, low = split(field)
        parts[0:TILE, :] = high
        parts[TILE : 2 * TILE, :] = low

        def sample(i, comp=comp):
            part = pl.ds(pl.multiple_of(i * turn, turn), turn)
            cells = lax.broadcasted_iota(jnp.int32, (TILE, turn), 0)
            near = jnp.dot(parts[...], on_rows[:, part], preferred_element_type=f32)
            near = near[0:TILE] + near[TILE : 2 * TILE]
            kick = jnp.sum(
                jnp.where(cells == col_ref[:, part], near, f32(0)), axis=0, keepdims=True
            )
            out_ref[comp : comp + 1, part] = momenta_ref[comp : comp + 1, part] + kick

        each(0, count // turn, sample)

    for exchange in (EX_A, EX_B, EX_Z):
        all_of(exchange).wait_send()
    for comp in range(2):
        for exchange in (EX_C, EX_P, EX_D):
            all_of(exchange, comp).wait_send()


def shards(cell_row, cell_col, weights, momenta):
    count = cell_row.shape[1]
    dma = pltpu.SemaphoreType.DMA
    base = base_tables()
    kicked = pl.pallas_call(
        collide_kernel,
        out_shape=jax.ShapeDtypeStruct((2, count), f32),
        in_specs=[pl.BlockSpec(memory_space=pltpu.HBM)] * 5,
        out_specs=pl.BlockSpec(memory_space=pltpu.VMEM),
        scratch_shapes=[
            pltpu.VMEM((1, count), jnp.int32),
            pltpu.VMEM((1, count), jnp.int32),
            pltpu.VMEM((1, count), f32),
            pltpu.VMEM((2, count), f32),
            pltpu.VMEM(base.shape, f32),
            pltpu.VMEM((TILE, count), bf16),
            pltpu.VMEM((2 * TILE, TILE), f32),
            pltpu.VMEM((PLANE, SHARE, TILE), f32),
            pltpu.VMEM((2, BLOCKS, TILE, TILE), bf16),
            pltpu.VMEM((TILE, TILE), bf16),
            pltpu.VMEM((TILE, TILE), bf16),
            pltpu.VMEM((PLANE, SHARE, TILE), f32),
            pltpu.VMEM((PLANE, SHARE, HALF), f32),
            pltpu.VMEM((PLANE, SHARE, HALF), f32),
            pltpu.VMEM((RING, SHARE, TILE), f32),
            pltpu.VMEM((RING, SHARE, TILE), f32),
            pltpu.VMEM((2, BLOCKS, SHARE, TILE), f32),
            pltpu.VMEM((2, RING, SHARE, TILE), f32),
            pltpu.VMEM((2, RING, SHARE, TILE), f32),
            pltpu.VMEM((2, PLANE, SHARE, HALF), f32),
            pltpu.VMEM((2, PLANE, SHARE, HALF), f32),
            pltpu.VMEM((2, BLOCKS, SHARE, TILE), f32),
            pltpu.VMEM((2, PLANE, SHARE, TILE), f32),
            pltpu.VMEM((2 * TILE, TILE), bf16),
            dma((5,)), dma((EXCHANGES,)), dma((EXCHANGES,)),
        ],
        compiler_params=pltpu.CompilerParams(
            vmem_limit_bytes=48 * 1024 * 1024, collective_id=0, has_side_effects=True
        ),
        name="collide",
    )(
        *[
            pltpu.with_memory_space_constraint(array, pltpu.HBM)
            for array in (cell_row, cell_col, weights, momenta[0], jnp.asarray(base))
        ]
    )
    return kicked[None]


def solution(mesh):
    placed = (
        P("beam", ("tx", "ty", "dom")),
        P("beam", ("tx", "ty", "dom")),
        P("beam", ("tx", "ty", "dom")),
        P("beam", None, ("tx", "ty", "dom")),
    )
    return jax.shard_map(
        shards,
        mesh=mesh,
        in_specs=placed,
        out_specs=P("beam", None, ("tx", "ty", "dom")),
        check_vma=False,
    )
```
